256 devices in a mesh: ctx: 16 (over z, core), row: 4 (over y), col: 4 (over x).
Axes of the slice: x: 4, y: 4, z: 8, core: 2. Of those that a mesh axis runs over, the one named last changes fastest.
Arguments:
- output_grad: bfloat16 [8192, 8192], P('ctx', ('row', 'col')), may hold values from -6 to 6
- conv_out: bfloat16 [8192, 8192], P('ctx', ('row', 'col')), may hold values from -9 to 9
- input_mix: bfloat16 [8192, 4, 256], P('ctx'), may hold values from -0.15625 to 0.15625
- output_mix: bfloat16 [8192, 4, 256], P('ctx'), may hold values from -1 to 1
- step_size: float32 [128, 8192], P(('row', 'col'), 'ctx'), may hold values from 0.5 to 2
- log_decay: float32 [128, 8192], P(('row', 'col'), 'ctx'), may hold values from -2.1 to 0, as said below
- skip_gain: float32 [128], P(('row', 'col')), may hold values from 0.5 to 2
- conv_weight: float32 [4, 8192], P(None, ('row', 'col')), may hold values from -3 to 3
- later_grad: float32 [128, 64, 256], P(('row', 'col')), may hold values from -32 to 32
- proj_weight: bfloat16 [8192, 8192], P('col', 'row'), may hold values from -0.0625 to 0.0625
Outputs:
- hidden_grad: bfloat16 [8192, 8192], P('ctx', ('col', 'row'))
- x_grad: bfloat16 [8192, 8192], P('ctx', ('row', 'col'))
- state_grad: float32 [16, 128, 64, 256], P('ctx', ('row', 'col'))
The draws below stay inside these ranges and needn't reach their ends.
Inputs may be any that keep to these rules, and one draw needn't show every extreme that they name: `log_decay`: the forward pass's log decay of each head at each token.
All inputs are finite; a program needn't handle non-finite values.
Results may differ from the reference program's by a relative error of at most 0.022.
Values may be sent and summed in bfloat16 or wider, within the bound.
No kernel may reach another device: no remote copies, remote signals or barrier semaphores. Data moves between devices by JAX's collectives and lax.ppermute only.
A program may use at most 128 MiB of HBM per device.

```python
import math
import jax
import jax.numpy as jnp
from jax import lax

D = 8192
HEAD_COUNT = 128
HD = 64
NS = 256
HPG = 32
KW = 4
BLOCK_TOKENS = 512
WINDOW_TOKENS = 8192
P_SIZE = 8192
G = 4
N_CTX = 16


def draw_log_decay(key, part):
    key_rows = jax.random.split(key, 9)
    share = 0.5
    slow_heads = jax.random.uniform(key_rows[0], (HEAD_COUNT, 1)) < share
    quiet_rate = jnp.exp(jax.random.uniform(key_rows[1], (HEAD_COUNT, 1), minval=math.log(0.05), maxval=math.log(0.3))) / BLOCK_TOKENS
    slow_rate = jnp.exp(jax.random.uniform(key_rows[2], (HEAD_COUNT, 1), minval=math.log(0.05), maxval=math.log(0.3))) / WINDOW_TOKENS
    base_rate = jnp.where(slow_heads, slow_rate, quiet_rate)
    stochastic_nudge = jnp.exp(jax.random.uniform(key_rows[3], (HEAD_COUNT, WINDOW_TOKENS), minval=math.log(0.5), maxval=math.log(2.0)))
    factors = jnp.exp(jax.random.uniform(key_rows[4], (N_CTX,), minval=math.log(0.5), maxval=math.log(2.0)))
    segment_scaling_factor = jnp.repeat(factors, BLOCK_TOKENS)
    gentle_portion = -base_rate * stochastic_nudge * segment_scaling_factor[None, :]
    surge_start = jax.random.randint(key_rows[7], (HEAD_COUNT, N_CTX), BLOCK_TOKENS // 2, BLOCK_TOKENS - 7)
    starting_points = jnp.repeat(surge_start, BLOCK_TOKENS, axis=1)
    offset_within_block = jnp.arange(WINDOW_TOKENS) % BLOCK_TOKENS
    inside_surge = (offset_within_block[None, :] >= starting_points) & (offset_within_block[None, :] < starting_points + 8)
    surge_depth = jnp.exp(jax.random.uniform(key_rows[8], (HEAD_COUNT, WINDOW_TOKENS), minval=math.log(0.75), maxval=math.log(1.5)))
    rapid_portion = jnp.where(inside_surge, -surge_depth, gentle_portion)
    head_values = jnp.where(slow_heads, gentle_portion, rapid_portion)
    marked_locations = jax.random.randint(key_rows[5], (3,), 0, WINDOW_TOKENS)
    objective_numbers = jax.random.uniform(key_rows[6], (3,), minval=0.2, maxval=0.4)
    token_places = jnp.arange(WINDOW_TOKENS)
    spike_occurrences = jnp.sum(jnp.where(token_places[None, :] == marked_locations[:, None], jnp.log(1.0 - objective_numbers)[:, None], 0.0), axis=0)
    return (head_values + spike_occurrences[None, :]).astype(jnp.float32)


def block_levels(own_key, dims, cuts, least, largest):
    factor_of = 1.0
    for axis_at, blocks in cuts:
        steps = jax.random.uniform(jax.random.fold_in(jax.random.fold_in(own_key, 6), axis_at), (blocks,), jnp.float32, least / len(cuts), largest / len(cuts))
        factor_of = factor_of * jnp.repeat(jnp.exp(steps), dims[axis_at] // blocks).reshape((-1,) + (1,) * (len(dims) - 1 - axis_at))
    return factor_of


def bell_draw(rng, shape, deviation, reach, cuts=(), kind=jnp.bfloat16):
    drawn = jax.random.normal(rng, shape, jnp.float32) * deviation
    if len(cuts) > 0:
        drawn = block_levels(rng, shape, cuts, -0.22, 0.18) * drawn
    return jnp.clip(drawn, min=-reach, max=reach).astype(kind)


def setup_inputs(seed: int = 0) -> dict:
    key_of = jax.random.split(jax.random.key(seed), 11)
    return {
        "output_grad": bell_draw(key_of[0], (WINDOW_TOKENS, P_SIZE), 1.0, 6.0, ((0, 16), (1, 16))),
        "conv_out": bell_draw(key_of[1], (WINDOW_TOKENS, P_SIZE), 1.5, 9.0, ((0, 16), (1, 16))),
        "input_mix": bell_draw(key_of[2], (WINDOW_TOKENS, G, NS), (WINDOW_TOKENS ** -0.5), 0.15625, ((0, 16),)),
        "output_mix": bell_draw(key_of[3], (WINDOW_TOKENS, G, NS), (NS ** -0.5), 1.0, ((0, 16),)),
        "step_size": jnp.clip(jnp.exp(math.log(2.0) - 1.3862944 * jax.random.uniform(key_of[4], (HEAD_COUNT, WINDOW_TOKENS), jnp.float32) ** block_levels(key_of[4], (HEAD_COUNT, WINDOW_TOKENS), ((0, 16), (1, 16)), -0.2, 0.2)), 0.5, 2.0),
        "log_decay": draw_log_decay(jax.random.fold_in(key_of[10], 71), 0),
        "skip_gain": jnp.clip(jnp.exp(math.log(2.0) - 1.3862944 * jax.random.uniform(key_of[6], (HEAD_COUNT,), jnp.float32) ** block_levels(key_of[6], (HEAD_COUNT,), ((0, 16),), -0.2, 0.2)), 0.5, 2.0),
        "conv_weight": bell_draw(key_of[7], (KW, P_SIZE), 0.5, 3.0, ((1, 16),), jnp.float32),
        "later_grad": bell_draw(key_of[8], (HEAD_COUNT, HD, NS), ((WINDOW_TOKENS / NS) ** 0.5), 32.0, ((0, 16),), jnp.float32),
        "proj_weight": bell_draw(key_of[9], (D, P_SIZE), P_SIZE ** -0.5, 0.0625, ((0, 4), (1, 4))),
    }


def reference(output_grad, conv_out, input_mix, output_mix, step_size, log_decay, skip_gain, conv_weight, later_grad, proj_weight):
    per_head = output_grad.reshape(WINDOW_TOKENS, HEAD_COUNT, HD)
    group_of = jnp.arange(HEAD_COUNT) // HPG
    positions = jnp.arange(BLOCK_TOKENS)
    causal = positions[None, :] >= positions[:, None]

    def one_block(carried, block_index):
        start = (block_index * BLOCK_TOKENS).astype(jnp.int32)
        grads = lax.dynamic_slice_in_dim(per_head, start, BLOCK_TOKENS, 0).astype(jnp.float32)
        write_rows = lax.dynamic_slice_in_dim(input_mix, start, BLOCK_TOKENS, 0).astype(jnp.float32)
        read_rows = lax.dynamic_slice_in_dim(output_mix, start, BLOCK_TOKENS, 0).astype(jnp.float32)
        decay_rows = lax.dynamic_slice_in_dim(log_decay, start, BLOCK_TOKENS, 1)
        steps_here = lax.dynamic_slice_in_dim(step_size, start, BLOCK_TOKENS, 1)
        cumulative = jnp.cumsum(decay_rows, axis=1)
        block_end = cumulative[:, -1]
        scores = jnp.einsum("tgn,sgn->gts", write_rows, read_rows)
        head_scores = scores[group_of]
        offsets = cumulative[:, None, :] - cumulative[:, :, None]
        mixing = (jnp.exp(jnp.where(causal[None], offsets, -jnp.inf)) * head_scores).astype(jnp.bfloat16)
        intra = jnp.einsum("hts,shd->thd", mixing.astype(jnp.float32), grads)
        weighted = (jnp.exp(cumulative).T[:, :, None] * grads).astype(jnp.bfloat16)
        head_reads = read_rows[:, group_of, :]
        head_writes = write_rows[:, group_of, :]
        block_sum = jnp.einsum("shd,shn->hdn", weighted.astype(jnp.float32), head_reads)
        inter = jnp.einsum("hdn,thn->thd", carried, head_writes, precision=lax.Precision.HIGHEST)
        inter = inter * jnp.exp(block_end[:, None] - cumulative).T[:, :, None]
        input_grad = steps_here.T[:, :, None] * (intra + inter) + skip_gain[None, :, None] * grads
        state_start = block_sum + jnp.exp(block_end)[:, None, None] * carried
        return state_start, (input_grad, state_start)

    order = jnp.arange(N_CTX - 1, -1, -1).astype(jnp.int32)
    unused, stacked = lax.scan(one_block, later_grad, order)
    input_grads = jnp.flip(stacked[0], axis=0).reshape(WINDOW_TOKENS, P_SIZE)
    state_grad = jnp.flip(stacked[1], axis=0)
    activated = conv_out.astype(jnp.float32)
    sigma = jax.nn.sigmoid(activated)
    pre_grad = (input_grads * sigma * (1.0 + activated * (1.0 - sigma))).astype(jnp.bfloat16)
    extended = jnp.concatenate([pre_grad.astype(jnp.float32), jnp.zeros((KW - 1, P_SIZE), jnp.float32)], axis=0)
    accum = jnp.zeros((WINDOW_TOKENS, P_SIZE), jnp.float32)
    for tap in range(KW):
        accum = accum + conv_weight[tap][None, :] * extended[tap:tap + WINDOW_TOKENS]
    x_grad = accum.astype(jnp.bfloat16)
    hidden_grad = jnp.dot(x_grad, proj_weight.T, preferred_element_type=jnp.float32).astype(jnp.bfloat16)
    return hidden_grad, x_grad, state_grad
```

```python
import jax
import jax.numpy as jnp
from jax import lax
from jax.experimental import pallas as pl
from jax.experimental.pallas import tpu as pltpu
from jax.sharding import PartitionSpec as P

HD = 64
HPG = 32
KW = 4
QUAD = 4
F32 = jnp.float32
BF16 = jnp.bfloat16
VMEM = pl.BlockSpec(memory_space=pltpu.VMEM)
SMEM = pl.BlockSpec(memory_space=pltpu.SMEM)


def struct(shape, dtype):
    return jax.ShapeDtypeStruct(shape, dtype)


def call(kernel, outs, args, scratch=(), flops=0, moved=0, smem=0):
    return pl.pallas_call(
        kernel,
        out_shape=outs,
        in_specs=[SMEM] * smem + [VMEM] * (len(args) - smem),
        out_specs=jax.tree.map(lambda unused: VMEM, outs),
        scratch_shapes=list(scratch),
        cost_estimate=pl.CostEstimate(flops=flops, bytes_accessed=moved, transcendentals=0),
        compiler_params=pltpu.CompilerParams(vmem_limit_bytes=40 << 20),
    )(*args)


def split3(value):
    high = value.astype(BF16)
    rest = value - high.astype(F32)
    middle = rest.astype(BF16)
    low = (rest - middle.astype(F32)).astype(BF16)
    return high, middle, low


def over_columns(per_head):
    heads = per_head.shape[0]
    stacked = jnp.concatenate([part.astype(F32) for part in split3(per_head)], axis=0).astype(BF16)
    row = lax.broadcasted_iota(jnp.int32, (3 * heads, heads * HD), 0)
    column = lax.broadcasted_iota(jnp.int32, (3 * heads, heads * HD), 1)
    picks = (lax.rem(row, heads) == column // HD).astype(F32).astype(BF16)
    return lax.dot_general(stacked, picks, (((0,), (0,)), ((), ())), preferred_element_type=F32)


def decay_rows(per_head):
    wide = jnp.broadcast_to(per_head, (per_head.shape[0], 256))
    high = wide.astype(BF16)
    low = (wide - high.astype(F32)).astype(BF16)
    return jnp.concatenate([high.astype(F32), low.astype(F32)], axis=0).astype(BF16)


def block_kernel(where, grad, reads, log_decay, sums, cumulative, decays, one, two, three):
    heads, tokens = log_decay.shape
    part = HD // QUAD
    total = log_decay[...]
    lane = lax.broadcasted_iota(jnp.int32, (heads, tokens), 1)
    step = 1
    while step < tokens:
        total = total + jnp.where(lane >= step, pltpu.roll(total, step, 1), 0.0)
        step *= 2
    cumulative[...] = total
    last = jnp.exp(total[:, tokens - 1 : tokens])
    decays[...] = jnp.broadcast_to(last, decays.shape)
    weighted = (over_columns(jnp.exp(total)) * grad[...].astype(F32)).astype(BF16)
    sums[...] = lax.dot_general(
        weighted, reads[...], (((0,), (0,)), ((), ())), preferred_element_type=F32
    )
    rows = decay_rows(last)
    me = where[0]
    for flip, sent in ((1, one), (2, two), (3, three)):
        quarter = jnp.bitwise_xor(me, flip)
        for head in range(heads):
            start = pl.multiple_of(head * HD + quarter * part, part)
            sent[head] = sums[pl.ds(start, part), :].astype(BF16)
        sent[heads] = rows


def intra_kernel(
    grad, writes, reads, cumulative, step_size, skip_row, conv_out, fixed, slope, scores, steps
):
    heads, tokens = cumulative.shape
    half = tokens // 2
    scores[...] = lax.dot_general(
        writes[...], reads[...], (((1,), (1,)), ((), ())), preferred_element_type=F32
    )
    total = cumulative[...]
    columns = jnp.transpose(total)
    steps[...] = over_columns(step_size[...])
    slope[...] = over_columns(
        step_size[...] * jnp.exp(total[:, tokens - 1 : tokens] - total)
    )
    causal = lax.broadcasted_iota(jnp.int32, (half, half), 1) >= lax.broadcasted_iota(
        jnp.int32, (half, half), 0
    )
    lane = lax.broadcasted_iota(jnp.int32, (half, 2 * HD), 1)
    for pair in range(heads // 2):
        span = slice(pair * 2 * HD, (pair + 1) * 2 * HD)
        for at in range(2):
            rows = slice(at * half, (at + 1) * half)
            both = []
            for head in (2 * pair, 2 * pair + 1):
                own = columns[rows, head : head + 1]
                offsets = total[head : head + 1, rows] - own
                mixing = (
                    jnp.exp(jnp.where(causal, offsets, -jnp.inf)) * scores[rows, rows]
                ).astype(BF16)
                sums = jnp.dot(mixing, grad[rows, span], preferred_element_type=F32)
                if at == 0:
                    later = slice(half, tokens)
                    mixing = (
                        jnp.exp(total[head : head + 1, later] - own) * scores[rows, later]
                    ).astype(BF16)
                    sums = sums + jnp.dot(mixing, grad[later, span], preferred_element_type=F32)
                both.append(sums)
            intra = jnp.where(lane < HD, both[0], both[1])
            activated = conv_out[rows, span].astype(F32)
            sigma = 1.0 / (1.0 + jnp.exp(-activated))
            gate = sigma * (1.0 + activated * (1.0 - sigma))
            fixed[rows, span] = gate * (
                steps[rows, span] * intra + skip_row[:, span] * grad[rows, span].astype(F32)
            )
            slope[rows, span] = gate * slope[rows, span]


def gather_quad(me, sums, decays, received, values, scales):
    heads = decays.shape[0]
    part = HD // QUAD
    for head in range(heads):
        start = pl.multiple_of(head * HD + me * part, part)
        values[me, head] = sums[pl.ds(start, part), :]
    scales[me] = decays[...]
    for flip, came in enumerate(received, 1):
        other = jnp.bitwise_xor(me, flip)
        for head in range(heads):
            values[other, head] = came[head].astype(F32)
        tail = came[heads].astype(F32)
        scales[other] = tail[:heads] + tail[heads:]


def quad_kernel(where, sums, decays, one, two, three, sent, values, scales):
    heads = decays.shape[0]
    gather_quad(where[0], sums, decays, (one, two, three), values, scales)
    for head in range(heads):
        total = values[3, head]
        for block in (2, 1, 0):
            total = values[block, head] + scales[block][head : head + 1] * total
        sent[head] = total.astype(BF16)
    product = scales[0] * scales[1] * scales[2] * scales[3]
    high = product.astype(BF16).astype(F32)
    sent[heads] = jnp.concatenate([high, product - high], axis=0).astype(BF16)


def carry_kernel(
    where, sums, decays, one, two, three, near, middle, far, later, own, first, second, third,
    values, scales, carries,
):
    heads = decays.shape[0]
    part = HD // QUAD
    me, quad = where[0], where[1]
    gather_quad(me, sums, decays, (one, two, three), values, scales)
    jumps = []
    for ahead, came in ((3, far), (2, middle), (1, near)):
        tail = came[heads].astype(F32)
        present = jnp.full(decays.shape, quad + ahead, jnp.int32) < QUAD
        jumps.append((came, jnp.where(present, tail[:heads] + tail[heads:], 1.0)))
    for head in range(heads):
        start = pl.multiple_of(head * HD + me * part, part)
        carry = later[pl.ds(start, part), :]
        for came, scale in jumps:
            carry = came[head].astype(F32) + scale[head : head + 1] * carry
        carries[3, head] = carry
        for block in (3, 2, 1):
            carry = values[block, head] + scales[block][head : head + 1] * carry
            carries[block - 1, head] = carry
    for head in range(heads):
        own[head] = carries[me, head]
        for flip, sent in ((1, first), (2, second), (3, third)):
            sent[head] = carries[jnp.bitwise_xor(me, flip), head].astype(BF16)


def join_kernel(
    where, sums, decays, own, first, second, third, writes, fixed, slope, taps,
    state, rim, chunk, rest, carried, pre,
):
    heads = decays.shape[0]
    part = HD // QUAD
    tokens = fixed.shape[0]
    half = tokens // 2
    me = where[0]
    for flip, came in ((0, own), (1, first), (2, second), (3, third)):
        quarter = jnp.bitwise_xor(me, flip)
        for head in range(heads):
            spot = pl.ds(pl.multiple_of(head * HD + quarter * part, part), part)
            value = came[head].astype(F32)
            state[spot, :] = sums[spot, :] + decays[head : head + 1] * value
            carried[spot, :] = value.astype(BF16)
    inter = lax.dot_general(
        writes[...], carried[...], (((1,), (1,)), ((), ())), preferred_element_type=F32
    )
    rounded = (fixed[...] + slope[...] * inter).astype(BF16)
    rim[...] = rounded[:16]
    rest[...] = rounded[half:]
    pre[...] = rounded[: half + 16].astype(F32)
    total = taps[0:1] * pre[0:half]
    for tap in range(1, KW):
        total = total + taps[tap : tap + 1] * pre[tap : tap + half]
    chunk[...] = total.astype(BF16)


def tail_kernel(rest, rim, chunk, taps, last, whole, pre):
    half = rest.shape[0]
    pre[:half] = rest[...].astype(F32)
    pre[half:] = rim[...].astype(F32)
    total = taps[0:1] * pre[0:half]
    for tap in range(1, KW):
        total = total + taps[tap : tap + 1] * pre[tap : tap + half]
    rounded = total.astype(BF16)
    last[...] = rounded
    whole[:half] = chunk[...]
    whole[half:] = rounded


def product_kernel(where, own, behind, ahead, across, weight, kept, up, down, over):
    row, column = where[2], where[3]
    width = own.shape[1]
    for place, out in ((2, over), (1, up), (3, down), (0, kept)):
        spot = pl.ds(pl.multiple_of(lax.rem(row + place, 4) * width, width), width)
        total = None
        for source, piece in ((0, own), (3, behind), (1, ahead), (2, across)):
            at = pl.ds(pl.multiple_of(lax.rem(column + source, 4) * width, width), width)
            term = lax.dot_general(
                piece[...], weight[spot, at], (((1,), (1,)), ((), ())), preferred_element_type=F32
            )
            total = term if total is None else total + term
        out[...] = total.astype(out.dtype)


def flipped(value, flip):
    count = lax.axis_size("ctx")
    return lax.ppermute(value, "ctx", [(place, place ^ flip) for place in range(count)])


def earlier(value, steps):
    count = lax.axis_size("ctx")
    return lax.ppermute(value, "ctx", [(place, place - steps) for place in range(steps, count)])


def around(value, axis, steps):
    count = lax.axis_size(axis)
    return lax.ppermute(value, axis, [(place, (place + steps) % count) for place in range(count)])


def on_device(
    output_grad, conv_out, input_mix, output_mix, step_size, log_decay, skip_gain, conv_weight,
    later_grad, proj_weight,
):
    tokens, width = output_grad.shape
    heads = step_size.shape[0]
    states = input_mix.shape[2]
    half = tokens // 2
    part = HD // QUAD
    ctx, row, column = lax.axis_index("ctx"), lax.axis_index("row"), lax.axis_index("col")
    where = jnp.stack([ctx % QUAD, ctx // QUAD, row, column]).astype(jnp.int32)
    group = (row * lax.axis_size("col") + column) * heads // HPG
    reads = lax.dynamic_index_in_dim(output_mix, group, 1, keepdims=False)
    writes = lax.dynamic_index_in_dim(input_mix, group, 1, keepdims=False)
    later = later_grad.reshape(width, states)
    skip_row = jnp.repeat(skip_gain, HD)[None, :]

    message = struct((heads + 1, part, states), BF16)
    piece = struct((heads, part, states), BF16)
    wide = struct((width, states), F32)
    plane = struct((tokens, width), F32)
    sums, cumulative, decays, *out = call(
        block_kernel,
        (wide, struct((heads, tokens), F32), struct((heads, states), F32)) + (message,) * 3,
        (where, output_grad, reads, log_decay),
        flops=2 * tokens * width * states, moved=3 << 20, smem=1,
    )
    near = [flipped(value, flip) for flip, value in enumerate(out, 1)]
    fixed, slope = call(
        intra_kernel,
        (plane, plane),
        (output_grad, writes, reads, cumulative, step_size, skip_row, conv_out),
        scratch=(pltpu.VMEM((tokens, tokens), F32), pltpu.VMEM((tokens, width), F32)),
        flops=6 * tokens * tokens * width, moved=6 << 20,
    )
    quads = (
        pltpu.VMEM((QUAD, heads, part, states), F32),
        pltpu.VMEM((QUAD, heads, states), F32),
    )
    joined = call(
        quad_kernel, message, (where, sums, decays, *near), scratch=quads, moved=1 << 20, smem=1
    )
    beyond = [earlier(joined, QUAD * ahead) for ahead in (1, 2, 3)]
    own, *out = call(
        carry_kernel,
        (struct((heads, part, states), F32),) + (piece,) * 3,
        (where, sums, decays, *near, *beyond, later),
        scratch=quads + (pltpu.VMEM((QUAD, heads, part, states), F32),),
        moved=1 << 20, smem=1,
    )
    parts = [flipped(value, flip) for flip, value in enumerate(out, 1)]
    block = struct((half, width), BF16)
    state, rim, chunk, rest = call(
        join_kernel,
        (wide, struct((16, width), BF16), block, block),
        (where, sums, decays, own, *parts, writes, fixed, slope, conv_weight),
        scratch=(pltpu.VMEM((width, states), BF16), pltpu.VMEM((half + 16, width), F32)),
        flops=2 * tokens * width * states, moved=4 << 20, smem=1,
    )
    rim = earlier(rim, 1)
    gathered = [around(chunk, "col", steps) for steps in (2, 1, -1)]
    last, x_grad = call(
        tail_kernel,
        (block, struct((tokens, width), BF16)),
        (rest, rim, chunk, conv_weight),
        scratch=(pltpu.VMEM((half + 16, width), F32),),
        moved=1 << 20,
    )
    gathered_last = [around(last, "col", steps) for steps in (2, 1, -1)]

    def product(mine, others):
        across, behind, ahead = others
        kept, up, down, over = call(
            product_kernel,
            (struct((half, width), F32), block, block, block),
            (where, mine, behind, ahead, across, proj_weight),
            flops=2 * half * proj_weight.size, moved=10 << 20, smem=1,
        )
        return kept, [around(over, "row", 2), around(up, "row", 1), around(down, "row", -1)]

    def total(kept, others):
        return (kept + sum(value.astype(F32) for value in others)).astype(BF16)

    first_sums = product(chunk, gathered)
    last_sums = product(last, gathered_last)
    hidden_grad = jnp.concatenate([total(*first_sums), total(*last_sums)], axis=0)
    return hidden_grad, x_grad, state.reshape(1, heads, HD, states)


def solution(mesh):
    return jax.shard_map(
        on_device,
        mesh=mesh,
        in_specs=(
            P("ctx", ("row", "col")),
            P("ctx", ("row", "col")),
            P("ctx", None, None),
            P("ctx", None, None),
            P(("row", "col"), "ctx"),
            P(("row", "col"), "ctx"),
            P(("row", "col")),
            P(None, ("row", "col")),
            P(("row", "col"), None, None),
            P("col", "row"),
        ),
        out_specs=(
            P("ctx", ("col", "row")),
            P("ctx", ("row", "col")),
            P("ctx", ("row", "col"), None, None),
        ),
        check_vma=False,
    )
```

```python
import jax
import jax.numpy as jnp
from jax import lax
from jax.experimental import pallas as pl
from jax.experimental.pallas import tpu as pltpu
from jax.sharding import PartitionSpec as P

HD = 64
HPG = 32
KW = 4
QUAD = 4
F32 = jnp.float32
BF16 = jnp.bfloat16
VMEM = pl.BlockSpec(memory_space=pltpu.VMEM)
SMEM = pl.BlockSpec(memory_space=pltpu.SMEM)
HBM = pl.BlockSpec(memory_space=pltpu.HBM)
FIRST = 256


def struct(shape, dtype):
    return jax.ShapeDtypeStruct(shape, dtype)


def call(kernel, outs, args, specs=(), scratch=()):
    return pl.pallas_call(
        kernel,
        out_shape=outs,
        in_specs=list(specs) + [VMEM] * (len(args) - len(specs)),
        out_specs=jax.tree.map(lambda unused: VMEM, outs),
        scratch_shapes=list(scratch),
        cost_estimate=pl.CostEstimate(flops=0, bytes_accessed=0, transcendentals=0),
        compiler_params=pltpu.CompilerParams(vmem_limit_bytes=40 << 20),
    )(*args)


def split3(value):
    high = value.astype(BF16)
    rest = value - high.astype(F32)
    middle = rest.astype(BF16)
    low = (rest - middle.astype(F32)).astype(BF16)
    return high, middle, low


def over_columns(per_head):
    heads = per_head.shape[0]
    stacked = jnp.concatenate([part.astype(F32) for part in split3(per_head)], axis=0).astype(BF16)
    row = lax.broadcasted_iota(jnp.int32, (3 * heads, heads * HD), 0)
    column = lax.broadcasted_iota(jnp.int32, (3 * heads, heads * HD), 1)
    picks = (lax.rem(row, heads) == column // HD).astype(F32).astype(BF16)
    return lax.dot_general(stacked, picks, (((0,), (0,)), ((), ())), preferred_element_type=F32)


def decay_rows(per_head):
    wide = jnp.broadcast_to(per_head, (per_head.shape[0], 256))
    high = wide.astype(BF16)
    low = (wide - high.astype(F32)).astype(BF16)
    return jnp.concatenate([high.astype(F32), low.astype(F32)], axis=0).astype(BF16)


def block_kernel(
    where, grad_hbm, reads, log_decay, sums, cumulative, decays, one, two, three, grad, total, arrived
):
    fetches = (
        pltpu.make_async_copy(log_decay, total, arrived.at[0]),
        pltpu.make_async_copy(grad_hbm, grad, arrived.at[1]),
    )
    for fetch in fetches:
        fetch.start()
    heads, tokens = total.shape
    part = HD // QUAD
    fetches[0].wait()
    running = total[...]
    lane = lax.broadcasted_iota(jnp.int32, (heads, tokens), 1)
    step = 1
    while step < tokens:
        running = running + jnp.where(lane >= step, pltpu.roll(running, step, 1), 0.0)
        step *= 2
    cumulative[...] = running
    last = jnp.exp(running[:, tokens - 1 : tokens])
    decays[...] = jnp.broadcast_to(last, decays.shape)
    spread = over_columns(jnp.exp(running))
    fetches[1].wait()
    weighted = (spread * grad[...].astype(F32)).astype(BF16)
    sums[...] = lax.dot_general(
        weighted, reads[...], (((0,), (0,)), ((), ())), preferred_element_type=F32
    )
    rows = decay_rows(last)
    me = where[0]
    for flip, sent in ((1, one), (2, two), (3, three)):
        quarter = jnp.bitwise_xor(me, flip)
        for head in range(heads):
            start = pl.multiple_of(head * HD + quarter * part, part)
            sent[head] = sums[pl.ds(start, part), :].astype(BF16)
        sent[heads] = rows


def intra_kernel(
    where, skips, grad_hbm, conv_hbm, step_hbm, later_hbm, writes, reads, cumulative, after,
    fixed, slope, quarter, scores, steps, grad, conv_out, step_size, later, arrived,
):
    fetches = [
        pltpu.make_async_copy(source, target, arrived.at[place])
        for place, (source, target) in enumerate(
            ((step_hbm, step_size), (grad_hbm, grad), (conv_hbm, conv_out), (later_hbm, later))
        )
    ]
    for fetch in fetches:
        fetch.start()
    heads, tokens = cumulative.shape
    part = HD // QUAD
    half = tokens // 2
    scores[...] = lax.dot_general(
        writes[...], reads[...], (((1,), (1,)), ((), ())), preferred_element_type=F32
    )
    total = cumulative[...]
    columns = jnp.transpose(total)
    fetches[0].wait()
    steps[...] = over_columns(step_size[...])
    slope[...] = over_columns(
        step_size[...] * jnp.exp(total[:, tokens - 1 : tokens] - total)
    )
    causal = lax.broadcasted_iota(jnp.int32, (half, half), 1) >= lax.broadcasted_iota(
        jnp.int32, (half, half), 0
    )
    lane = lax.broadcasted_iota(jnp.int32, (half, 2 * HD), 1)
    for fetch in fetches[1:]:
        fetch.wait()
    for head in range(heads):
        start = pl.multiple_of(head * HD + where[0] * part, part)
        quarter[head] = later[pl.ds(start, part), :]
    for pair in range(heads // 2):
        span = slice(pair * 2 * HD, (pair + 1) * 2 * HD)
        skip = jnp.where(lane < HD, skips[2 * pair], skips[2 * pair + 1])
        for at in range(2):
            rows = slice(at * half, (at + 1) * half)
            both = []
            for head in (2 * pair, 2 * pair + 1):
                own = columns[rows, head : head + 1]
                offsets = total[head : head + 1, rows] - own
                mixing = (
                    jnp.exp(jnp.where(causal, offsets, -jnp.inf)) * scores[rows, rows]
                ).astype(BF16)
                sums = jnp.dot(mixing, grad[rows, span], preferred_element_type=F32)
                if at == 0:
                    rest = slice(half, tokens)
                    mixing = (
                        jnp.exp(total[head : head + 1, rest] - own) * scores[rows, rest]
                    ).astype(BF16)
                    sums = sums + jnp.dot(mixing, grad[rest, span], preferred_element_type=F32)
                both.append(sums)
            intra = jnp.where(lane < HD, both[0], both[1])
            activated = conv_out[rows, span].astype(F32)
            sigma = 1.0 / (1.0 + jnp.exp(-activated))
            gate = sigma * (1.0 + activated * (1.0 - sigma))
            fixed[rows, span] = gate * (
                steps[rows, span] * intra + skip * grad[rows, span].astype(F32)
            )
            slope[rows, span] = gate * slope[rows, span]


def gather_quad(me, sums, decays, received, values, scales):
    heads = decays.shape[0]
    part = HD // QUAD
    for head in range(heads):
        start = pl.multiple_of(head * HD + me * part, part)
        values[me, head] = sums[pl.ds(start, part), :]
    scales[me] = decays[...]
    for flip, came in enumerate(received, 1):
        other = jnp.bitwise_xor(me, flip)
        for head in range(heads):
            values[other, head] = came[head].astype(F32)
        tail = came[heads].astype(F32)
        scales[other] = tail[:heads] + tail[heads:]


def quad_kernel(where, sums, decays, one, two, three, after, sent, values, scales):
    heads = decays.shape[0]
    gather_quad(where[0], sums, decays, (one, two, three), values, scales)
    for head in range(heads):
        total = values[3, head]
        for block in (2, 1, 0):
            total = values[block, head] + scales[block][head : head + 1] * total
        sent[head] = total.astype(BF16)
    product = scales[0] * scales[1] * scales[2] * scales[3]
    high = product.astype(BF16).astype(F32)
    sent[heads] = jnp.concatenate([high, product - high], axis=0).astype(BF16)


def carry_kernel(
    where, sums, decays, one, two, three, far, near, middle, later, own, first, second, third,
    values, scales, carries,
):
    heads = decays.shape[0]
    me, quad = where[0], where[1]
    gather_quad(me, sums, decays, (one, two, three), values, scales)
    jumps = []
    for ahead, came in ((3, far), (2, middle), (1, near)):
        tail = came[heads].astype(F32)
        present = jnp.full(decays.shape, quad + ahead, jnp.int32) < QUAD
        jumps.append((came, jnp.where(present, tail[:heads] + tail[heads:], 1.0)))
    for head in range(heads):
        carry = later[head]
        for came, scale in jumps:
            carry = came[head].astype(F32) + scale[head : head + 1] * carry
        carries[3, head] = carry.astype(BF16)
        for block in (3, 2, 1):
            carry = values[block, head] + scales[block][head : head + 1] * carry
            carries[block - 1, head] = carry.astype(BF16)
    for flip, sent in ((0, own), (1, first), (2, second), (3, third)):
        sent[...] = carries[jnp.bitwise_xor(me, flip)]


def taps_sum(pre, taps, start, count):
    total = taps[0:1] * pre[start : start + count]
    for tap in range(1, KW):
        total = total + taps[tap : tap + 1] * pre[start + tap : start + tap + count]
    return total.astype(BF16)


def join_kernel(
    where, own, first, second, third, writes, fixed, slope, taps, chunk, rim, rest, carried, pre
):
    heads = own.shape[0]
    part = HD // QUAD
    me = where[0]
    for flip, came in ((0, own), (1, first), (2, second), (3, third)):
        quarter = jnp.bitwise_xor(me, flip)
        for head in range(heads):
            spot = pl.ds(pl.multiple_of(head * HD + quarter * part, part), part)
            carried[spot, :] = came[head]
    count = chunk.shape[0]
    inter = lax.dot_general(
        writes[...], carried[...], (((1,), (1,)), ((), ())), preferred_element_type=F32
    )
    rounded = (fixed[...] + slope[...] * inter).astype(BF16)
    rim[...] = rounded[:16]
    rest[...] = rounded[count:]
    pre[...] = rounded[: count + 16].astype(F32)
    chunk[...] = taps_sum(pre, taps, 0, count)


def tail_kernel(rest, rim, taps, chunk, pre):
    count = rest.shape[0]
    pre[:count] = rest[...].astype(F32)
    pre[count:] = rim[...].astype(F32)
    chunk[...] = taps_sum(pre, taps, 0, count)


def output_kernel(sums, decays, carried, head, last, after, state, x_grad):
    for at in range(decays.shape[0]):
        spot = slice(at * HD, (at + 1) * HD)
        state[spot] = sums[spot] + decays[at : at + 1] * carried[spot].astype(F32)
    x_grad[: head.shape[0]] = head[...]
    x_grad[head.shape[0] :] = last[...]


def product_kernel(where, own, near, far, weight, after, total):
    column = where[3]
    width = own.shape[1]
    for place in range(4):
        spot = slice(place * width, (place + 1) * width)
        sums = None
        for flip, piece in ((0, own), (1, near), (3, far)):
            source = jnp.bitwise_xor(column, flip)
            at = pl.ds(pl.multiple_of(source * width, width), width)
            term = lax.dot_general(
                piece[...], weight[spot, at], (((1,), (1,)), ((), ())), preferred_element_type=F32
            )
            sums = term if sums is None else sums + term
        total[:, spot] = sums


def finish_kernel(where, across, weight, total, kept, near, far, over):
    row, column = where[2], where[3]
    width = across.shape[1]
    at = pl.ds(pl.multiple_of(jnp.bitwise_xor(column, 2) * width, width), width)
    for flip, out in ((2, over), (1, near), (3, far), (0, kept)):
        target = jnp.bitwise_xor(row, flip)
        spot = pl.ds(pl.multiple_of(target * width, width), width)
        term = lax.dot_general(
            across[...], weight[spot, at], (((1,), (1,)), ((), ())), preferred_element_type=F32
        )
        out[...] = (total[:, spot] + term).astype(out.dtype)


def earlier(value, steps):
    count = lax.axis_size("ctx")
    return lax.ppermute(value, "ctx", [(place, place - steps) for place in range(steps, count)])


def swapped(value, axis, flip):
    count = lax.axis_size(axis)
    return lax.ppermute(value, axis, [(place, place ^ flip) for place in range(count)])


def on_device(
    output_grad, conv_out, input_mix, output_mix, step_size, log_decay, skip_gain, conv_weight,
    later_grad, proj_weight,
):
    tokens, width = output_grad.shape
    heads = step_size.shape[0]
    states = input_mix.shape[2]
    part = HD // QUAD
    ctx, row, column = lax.axis_index("ctx"), lax.axis_index("row"), lax.axis_index("col")
    where = jnp.stack([ctx % QUAD, ctx // QUAD, row, column]).astype(jnp.int32)
    group = (row * lax.axis_size("col") + column) * heads // HPG
    reads = lax.dynamic_index_in_dim(output_mix, group, 1, keepdims=False)
    writes = lax.dynamic_index_in_dim(input_mix, group, 1, keepdims=False)
    later = later_grad.reshape(width, states)

    message = struct((heads + 1, part, states), BF16)
    piece = struct((heads, part, states), BF16)
    wide = struct((width, states), F32)
    plane = struct((tokens, width), F32)
    sums, cumulative, decays, *out = call(
        block_kernel,
        (wide, struct((heads, tokens), F32), struct((heads, states), F32)) + (message,) * 3,
        (where, output_grad, reads, log_decay),
        specs=(SMEM, HBM, VMEM, HBM),
        scratch=(
            pltpu.VMEM((tokens, width), BF16),
            pltpu.VMEM((heads, tokens), F32),
            pltpu.SemaphoreType.DMA((2,)),
        ),
    )
    near = [swapped(value, "ctx", flip) for flip, value in enumerate(out, 1)]
    quads = (
        pltpu.VMEM((QUAD, heads, part, states), F32),
        pltpu.VMEM((QUAD, heads, states), F32),
    )
    joined = call(
        quad_kernel, message, (where, sums, decays, *near, writes), specs=(SMEM,), scratch=quads,
    )
    far, middle, close = (earlier(joined, QUAD * ahead) for ahead in (3, 2, 1))
    fixed, slope, quarter = call(
        intra_kernel,
        (plane, plane, struct((heads, part, states), F32)),
        (where, skip_gain, output_grad, conv_out, step_size, later, writes, reads, cumulative)
        + (joined,),
        specs=(SMEM, SMEM, HBM, HBM, HBM, HBM),
        scratch=(
            pltpu.VMEM((tokens, tokens), F32),
            pltpu.VMEM((tokens, width), F32),
            pltpu.VMEM((tokens, width), BF16),
            pltpu.VMEM((tokens, width), BF16),
            pltpu.VMEM((heads, tokens), F32),
            pltpu.VMEM((width, states), F32),
            pltpu.SemaphoreType.DMA((4,)),
        ),
    )
    own, *out = call(
        carry_kernel,
        (piece,) * 4,
        (where, sums, decays, *near, far, close, middle, quarter),
        specs=(SMEM,),
        scratch=quads + (pltpu.VMEM((QUAD, heads, part, states), BF16),),
    )
    parts = [swapped(value, "ctx", flip) for flip, value in enumerate(out, 1)]
    blocks = [struct((count, width), BF16) for count in (FIRST, tokens - FIRST)]
    head, rim, rest, carried = call(
        join_kernel,
        (blocks[0], struct((16, width), BF16), blocks[1], struct((width, states), BF16)),
        (where, own, *parts, writes, fixed, slope, conv_weight),
        specs=(SMEM,),
        scratch=(pltpu.VMEM((FIRST + 16, width), F32),),
    )
    last = call(
        tail_kernel,
        blocks[1],
        (rest, earlier(rim, 1), conv_weight),
        scratch=(pltpu.VMEM((tokens - FIRST + 16, width), F32),),
    )
    sums_of, after = [], head
    for chunk in (head, last):
        near, far, across = (swapped(chunk, "col", flip) for flip in (1, 3, 2))
        block, held = struct(chunk.shape, BF16), struct(chunk.shape, F32)
        partial = call(
            product_kernel,
            struct((chunk.shape[0], proj_weight.shape[0]), F32),
            (where, chunk, near, far, proj_weight, after),
            specs=(SMEM,),
        )
        kept, near, far, over = call(
            finish_kernel,
            (held, block, block, block),
            (where, across, proj_weight, partial),
            specs=(SMEM,),
        )
        came = [swapped(value, "row", flip) for value, flip in ((near, 1), (far, 3), (over, 2))]
        sums_of.append(kept + sum(value.astype(F32) for value in came))
        after = kept
    state, x_grad = call(
        output_kernel,
        (wide, struct((tokens, width), BF16)),
        (sums, decays, carried, head, last, after),
    )
    hidden_grad = jnp.concatenate(sums_of, axis=0).astype(BF16)
    return hidden_grad, x_grad, state.reshape(1, heads, HD, states)


def solution(mesh):
    return jax.shard_map(
        on_device,
        mesh=mesh,
        in_specs=(
            P("ctx", ("row", "col")),
            P("ctx", ("row", "col")),
            P("ctx", None, None),
            P("ctx", None, None),
            P(("row", "col"), "ctx"),
            P(("row", "col"), "ctx"),
            P(("row", "col")),
            P(None, ("row", "col")),
            P(("row", "col"), None, None),
            P("col", "row"),
        ),
        out_specs=(
            P("ctx", ("col", "row")),
            P("ctx", ("row", "col")),
            P("ctx", ("row", "col"), None, None),
        ),
        check_vma=False,
    )
```

```python
import jax
import jax.numpy as jnp
from jax import lax
from jax.experimental import pallas as pl
from jax.experimental.pallas import tpu as pltpu
from jax.sharding import PartitionSpec as P

HD = 64
HPG = 32
KW = 4
QUAD = 4
F32 = jnp.float32
BF16 = jnp.bfloat16
VMEM = pl.BlockSpec(memory_space=pltpu.VMEM)
SMEM = pl.BlockSpec(memory_space=pltpu.SMEM)
HBM = pl.BlockSpec(memory_space=pltpu.HBM)
FIRST = 256


def struct(shape, dtype):
    return jax.ShapeDtypeStruct(shape, dtype)


def call(kernel, outs, args, specs=(), scratch=()):
    return pl.pallas_call(
        kernel,
        out_shape=outs,
        in_specs=list(specs) + [VMEM] * (len(args) - len(specs)),
        out_specs=jax.tree.map(lambda unused: VMEM, outs),
        scratch_shapes=list(scratch),
        cost_estimate=pl.CostEstimate(flops=0, bytes_accessed=0, transcendentals=0),
        compiler_params=pltpu.CompilerParams(vmem_limit_bytes=40 << 20),
    )(*args)


def split3(value):
    high = value.astype(BF16)
    rest = value - high.astype(F32)
    middle = rest.astype(BF16)
    low = (rest - middle.astype(F32)).astype(BF16)
    return high, middle, low


def over_columns(per_head):
    heads = per_head.shape[0]
    stacked = jnp.concatenate([part.astype(F32) for part in split3(per_head)], axis=0).astype(BF16)
    row = lax.broadcasted_iota(jnp.int32, (3 * heads, heads * HD), 0)
    column = lax.broadcasted_iota(jnp.int32, (3 * heads, heads * HD), 1)
    picks = (lax.rem(row, heads) == column // HD).astype(F32).astype(BF16)
    return lax.dot_general(stacked, picks, (((0,), (0,)), ((), ())), preferred_element_type=F32)


def decay_rows(per_head):
    wide = per_head
    high = wide.astype(BF16).astype(F32)
    return jnp.concatenate([high, wide - high], axis=1).astype(BF16)


def decays_of(rows):
    parts = rows.astype(F32)
    half = parts.shape[1] // 2
    total = parts[:, :half] + parts[:, half:]
    return jnp.concatenate([total, total], axis=1)


def block_kernel(
    where, grad_hbm, reads, log_decay, sums, cumulative, decays, one, two, three, grad, total, arrived
):
    fetches = (
        pltpu.make_async_copy(log_decay, total, arrived.at[0]),
        pltpu.make_async_copy(grad_hbm, grad, arrived.at[1]),
    )
    for fetch in fetches:
        fetch.start()
    heads, tokens = total.shape
    part = HD // QUAD
    fetches[0].wait()
    running = total[...]
    lane = lax.broadcasted_iota(jnp.int32, (heads, tokens), 1)
    step = 1
    while step < tokens:
        running = running + jnp.where(lane >= step, pltpu.roll(running, step, 1), 0.0)
        step *= 2
    cumulative[...] = running
    last = jnp.exp(running[:, tokens - 1 : tokens])
    decays[...] = jnp.broadcast_to(last, decays.shape)
    spread = over_columns(jnp.exp(running))
    fetches[1].wait()
    weighted = (spread * grad[...].astype(F32)).astype(BF16)
    sums[...] = lax.dot_general(
        weighted, reads[...], (((0,), (0,)), ((), ())), preferred_element_type=F32
    )
    rows = decay_rows(jnp.broadcast_to(last, (heads, decays.shape[1] // 2)))
    me = where[0]
    for flip, sent in ((1, one), (2, two), (3, three)):
        quarter = jnp.bitwise_xor(me, flip)
        for head in range(heads):
            start = pl.multiple_of(head * HD + quarter * part, part)
            sent[head * part : (head + 1) * part] = sums[pl.ds(start, part), :].astype(BF16)
        sent[heads * part :] = rows


def intra_kernel(
    where, skips, grad_hbm, conv_hbm, step_hbm, later_hbm, writes, reads, cumulative, after,
    fixed, slope, quarter, scores, steps, grad, conv_out, step_size, later, arrived,
):
    fetches = [
        pltpu.make_async_copy(source, target, arrived.at[place])
        for place, (source, target) in enumerate(
            ((step_hbm, step_size), (grad_hbm, grad), (conv_hbm, conv_out), (later_hbm, later))
        )
    ]
    for fetch in fetches:
        fetch.start()
    heads, tokens = cumulative.shape
    part = HD // QUAD
    half = tokens // 2
    scores[...] = lax.dot_general(
        writes[...], reads[...], (((1,), (1,)), ((), ())), preferred_element_type=F32
    )
    total = cumulative[...]
    columns = jnp.transpose(total)
    fetches[0].wait()
    steps[...] = over_columns(step_size[...])
    slope[...] = over_columns(
        step_size[...] * jnp.exp(total[:, tokens - 1 : tokens] - total)
    )
    causal = lax.broadcasted_iota(jnp.int32, (half, half), 1) >= lax.broadcasted_iota(
        jnp.int32, (half, half), 0
    )
    lane = lax.broadcasted_iota(jnp.int32, (half, 2 * HD), 1)
    for fetch in fetches[1:]:
        fetch.wait()
    for head in range(heads):
        start = pl.multiple_of(head * HD + where[0] * part, part)
        quarter[head] = later[pl.ds(start, part), :]
    for pair in range(heads // 2):
        span = slice(pair * 2 * HD, (pair + 1) * 2 * HD)
        skip = jnp.where(lane < HD, skips[2 * pair], skips[2 * pair + 1])
        for at in range(2):
            rows = slice(at * half, (at + 1) * half)
            both = []
            for head in (2 * pair, 2 * pair + 1):
                own = columns[rows, head : head + 1]
                offsets = total[head : head + 1, rows] - own
                mixing = (
                    jnp.exp(jnp.where(causal, offsets, -jnp.inf)) * scores[rows, rows]
                ).astype(BF16)
                sums = jnp.dot(mixing, grad[rows, span], preferred_element_type=F32)
                if at == 0:
                    rest = slice(half, tokens)
                    mixing = (
                        jnp.exp(total[head : head + 1, rest] - own) * scores[rows, rest]
                    ).astype(BF16)
                    sums = sums + jnp.dot(mixing, grad[rest, span], preferred_element_type=F32)
                both.append(sums)
            intra = jnp.where(lane < HD, both[0], both[1])
            activated = conv_out[rows, span].astype(F32)
            sigma = 1.0 / (1.0 + jnp.exp(-activated))
            gate = sigma * (1.0 + activated * (1.0 - sigma))
            fixed[rows, span] = gate * (
                steps[rows, span] * intra + skip * grad[rows, span].astype(F32)
            )
            slope[rows, span] = gate * slope[rows, span]


def gather_quad(me, sums, decays, received, values, scales):
    heads = decays.shape[0]
    part = HD // QUAD
    for head in range(heads):
        start = pl.multiple_of(head * HD + me * part, part)
        values[me, head] = sums[pl.ds(start, part), :]
    scales[me] = decays[...]
    for flip, came in enumerate(received, 1):
        other = jnp.bitwise_xor(me, flip)
        for head in range(heads):
            values[other, head] = came[head * part : (head + 1) * part].astype(F32)
        scales[other] = decays_of(came[heads * part :])


def quad_kernel(where, sums, decays, one, two, three, after, sent, values, scales):
    heads = decays.shape[0]
    part = HD // QUAD
    gather_quad(where[0], sums, decays, (one, two, three), values, scales)
    for head in range(heads):
        total = values[3, head]
        for block in (2, 1, 0):
            total = values[block, head] + scales[block][head : head + 1] * total
        sent[head * part : (head + 1) * part] = total.astype(BF16)
    product = scales[0] * scales[1] * scales[2] * scales[3]
    sent[heads * part :] = decay_rows(product[:, : product.shape[1] // 2])


def carry_kernel(
    where, sums, decays, one, two, three, far, near, middle, later, own, first, second, third,
    values, scales, carries,
):
    heads = decays.shape[0]
    part = HD // QUAD
    me, quad = where[0], where[1]
    gather_quad(me, sums, decays, (one, two, three), values, scales)
    jumps = []
    for ahead, came in ((3, far), (2, middle), (1, near)):
        present = jnp.full(decays.shape, quad + ahead, jnp.int32) < QUAD
        jumps.append((came, jnp.where(present, decays_of(came[heads * part :]), 1.0)))
    for head in range(heads):
        carry = later[head]
        for came, scale in jumps:
            sent = came[head * part : (head + 1) * part].astype(F32)
            carry = sent + scale[head : head + 1] * carry
        carries[3, head] = carry.astype(BF16)
        for block in (3, 2, 1):
            carry = values[block, head] + scales[block][head : head + 1] * carry
            carries[block - 1, head] = carry.astype(BF16)
    for flip, sent in ((0, own), (1, first), (2, second), (3, third)):
        sent[...] = carries[jnp.bitwise_xor(me, flip)]


def taps_sum(pre, taps, start, count):
    total = taps[0:1] * pre[start : start + count]
    for tap in range(1, KW):
        total = total + taps[tap : tap + 1] * pre[start + tap : start + tap + count]
    return total.astype(BF16)


def join_kernel(
    where, own, first, second, third, writes, fixed, slope, taps, chunk, rim, rest, carried, pre
):
    heads = own.shape[0]
    part = HD // QUAD
    me = where[0]
    for flip, came in ((0, own), (1, first), (2, second), (3, third)):
        quarter = jnp.bitwise_xor(me, flip)
        for head in range(heads):
            spot = pl.ds(pl.multiple_of(head * HD + quarter * part, part), part)
            carried[spot, :] = came[head]
    count = chunk.shape[0]
    inter = lax.dot_general(
        writes[...], carried[...], (((1,), (1,)), ((), ())), preferred_element_type=F32
    )
    rounded = (fixed[...] + slope[...] * inter).astype(BF16)
    rim[...] = rounded[:16]
    rest[...] = rounded[count:]
    pre[...] = rounded[: count + 16].astype(F32)
    chunk[...] = taps_sum(pre, taps, 0, count)


def tail_kernel(rest, rim, taps, chunk, pre):
    count = rest.shape[0]
    pre[:count] = rest[...].astype(F32)
    pre[count:] = rim[...].astype(F32)
    chunk[...] = taps_sum(pre, taps, 0, count)


def output_kernel(sums, decays, carried, head, last, after, state, x_grad):
    for at in range(decays.shape[0]):
        spot = slice(at * HD, (at + 1) * HD)
        state[spot] = sums[spot] + decays[at : at + 1] * carried[spot].astype(F32)
    x_grad[: head.shape[0]] = head[...]
    x_grad[head.shape[0] :] = last[...]


def product_kernel(where, own, far, near, weight, after, total):
    column = where[3]
    width = own.shape[1]
    for place in range(4):
        spot = slice(place * width, (place + 1) * width)
        sums = None
        for flip, piece in ((0, own), (1, near), (3, far)):
            source = jnp.bitwise_xor(column, flip)
            at = pl.ds(pl.multiple_of(source * width, width), width)
            term = lax.dot_general(
                piece[...], weight[spot, at], (((1,), (1,)), ((), ())), preferred_element_type=F32
            )
            sums = term if sums is None else sums + term
        total[:, spot] = sums


def finish_kernel(where, across, weight, total, kept, near, far, over):
    row, column = where[2], where[3]
    width = across.shape[1]
    at = pl.ds(pl.multiple_of(jnp.bitwise_xor(column, 2) * width, width), width)
    for flip, out in ((2, over), (1, near), (3, far), (0, kept)):
        target = jnp.bitwise_xor(row, flip)
        spot = pl.ds(pl.multiple_of(target * width, width), width)
        term = lax.dot_general(
            across[...], weight[spot, at], (((1,), (1,)), ((), ())), preferred_element_type=F32
        )
        out[...] = (total[:, spot] + term).astype(out.dtype)


def earlier(value, steps):
    count = lax.axis_size("ctx")
    return lax.ppermute(value, "ctx", [(place, place - steps) for place in range(steps, count)])


def swapped(value, axis, flip):
    count = lax.axis_size(axis)
    return lax.ppermute(value, axis, [(place, place ^ flip) for place in range(count)])


def on_device(
    output_grad, conv_out, input_mix, output_mix, step_size, log_decay, skip_gain, conv_weight,
    later_grad, proj_weight,
):
    tokens, width = output_grad.shape
    heads = step_size.shape[0]
    states = input_mix.shape[2]
    part = HD // QUAD
    ctx, row, column = lax.axis_index("ctx"), lax.axis_index("row"), lax.axis_index("col")
    where = jnp.stack([ctx % QUAD, ctx // QUAD, row, column]).astype(jnp.int32)
    group = (row * lax.axis_size("col") + column) * heads // HPG
    reads = lax.dynamic_index_in_dim(output_mix, group, 1, keepdims=False)
    writes = lax.dynamic_index_in_dim(input_mix, group, 1, keepdims=False)
    later = later_grad.reshape(width, states)

    message = struct((heads * part + heads, states), BF16)
    piece = struct((heads, part, states), BF16)
    wide = struct((width, states), F32)
    plane = struct((tokens, width), F32)
    sums, cumulative, decays, *out = call(
        block_kernel,
        (wide, struct((heads, tokens), F32), struct((heads, states), F32)) + (message,) * 3,
        (where, output_grad, reads, log_decay),
        specs=(SMEM, HBM, VMEM, HBM),
        scratch=(
            pltpu.VMEM((tokens, width), BF16),
            pltpu.VMEM((heads, tokens), F32),
            pltpu.SemaphoreType.DMA((2,)),
        ),
    )
    near = [swapped(value, "ctx", flip) for flip, value in enumerate(out, 1)]
    quads = (
        pltpu.VMEM((QUAD, heads, part, states), F32),
        pltpu.VMEM((QUAD, heads, states), F32),
    )
    joined = call(
        quad_kernel, message, (where, sums, decays, *near, writes), specs=(SMEM,), scratch=quads,
    )
    far, middle, close = (earlier(joined, QUAD * ahead) for ahead in (3, 2, 1))
    fixed, slope, quarter = call(
        intra_kernel,
        (plane, plane, struct((heads, part, states), F32)),
        (where, skip_gain, output_grad, conv_out, step_size, later, writes, reads, cumulative)
        + (joined,),
        specs=(SMEM, SMEM, HBM, HBM, HBM, HBM),
        scratch=(
            pltpu.VMEM((tokens, tokens), F32),
            pltpu.VMEM((tokens, width), F32),
            pltpu.VMEM((tokens, width), BF16),
            pltpu.VMEM((tokens, width), BF16),
            pltpu.VMEM((heads, tokens), F32),
            pltpu.VMEM((width, states), F32),
            pltpu.SemaphoreType.DMA((4,)),
        ),
    )
    own, *out = call(
        carry_kernel,
        (piece,) * 4,
        (where, sums, decays, *near, far, close, middle, quarter),
        specs=(SMEM,),
        scratch=quads + (pltpu.VMEM((QUAD, heads, part, states), BF16),),
    )
    parts = [swapped(value, "ctx", flip) for flip, value in enumerate(out, 1)]
    blocks = [struct((count, width), BF16) for count in (FIRST, tokens - FIRST)]
    head, rim, rest, carried = call(
        join_kernel,
        (blocks[0], struct((16, width), BF16), blocks[1], struct((width, states), BF16)),
        (where, own, *parts, writes, fixed, slope, conv_weight),
        specs=(SMEM,),
        scratch=(pltpu.VMEM((FIRST + 16, width), F32),),
    )
    last = call(
        tail_kernel,
        blocks[1],
        (rest, earlier(rim, 1), conv_weight),
        scratch=(pltpu.VMEM((tokens - FIRST + 16, width), F32),),
    )
    sums_of, after = [], head
    for chunk in (head, last):
        near, far, across = (swapped(chunk, "col", flip) for flip in (1, 3, 2))
        block, held = struct(chunk.shape, BF16), struct(chunk.shape, F32)
        partial = call(
            product_kernel,
            struct((chunk.shape[0], proj_weight.shape[0]), F32),
            (where, chunk, far, near, proj_weight, after),
            specs=(SMEM,),
        )
        kept, near, far, over = call(
            finish_kernel,
            (held, block, block, block),
            (where, across, proj_weight, partial),
            specs=(SMEM,),
        )
        came = [swapped(value, "row", flip) for value, flip in ((near, 1), (far, 3), (over, 2))]
        sums_of.append((kept, *came))
        after = kept
    state, x_grad = call(
        output_kernel,
        (wide, struct((tokens, width), BF16)),
        (sums, decays, carried, head, last, came[0]),
    )
    kept, *came = sums_of[-1]
    sums_of[-1] = lax.optimization_barrier((kept, *came, state))[:-1]
    sums_of = [kept + sum(value.astype(F32) for value in came) for kept, *came in sums_of]
    hidden_grad = jnp.concatenate(sums_of, axis=0).astype(BF16)
    return hidden_grad, x_grad, state.reshape(1, heads, HD, states)


def solution(mesh):
    return jax.shard_map(
        on_device,
        mesh=mesh,
        in_specs=(
            P("ctx", ("row", "col")),
            P("ctx", ("row", "col")),
            P("ctx", None, None),
            P("ctx", None, None),
            P(("row", "col"), "ctx"),
            P(("row", "col"), "ctx"),
            P(("row", "col")),
            P(None, ("row", "col")),
            P(("row", "col"), None, None),
            P("col", "row"),
        ),
        out_specs=(
            P("ctx", ("col", "row")),
            P("ctx", ("row", "col")),
            P("ctx", ("row", "col"), None, None),
        ),
        check_vma=False,
    )
```

```python
import functools

import jax
import jax.numpy as jnp
from jax import lax
from jax.experimental import pallas as pl
from jax.experimental.pallas import tpu as pltpu
from jax.sharding import PartitionSpec as P

HD = 64
HPG = 32
KW = 4
QUAD = 4
F32 = jnp.float32
BF16 = jnp.bfloat16
VMEM = pl.BlockSpec(memory_space=pltpu.VMEM)
SMEM = pl.BlockSpec(memory_space=pltpu.SMEM)
HBM = pl.BlockSpec(memory_space=pltpu.HBM)
FIRST = 256


def struct(shape, dtype):
    return jax.ShapeDtypeStruct(shape, dtype)


def call(kernel, outs, args, specs=(), scratch=()):
    return pl.pallas_call(
        kernel,
        out_shape=outs,
        in_specs=list(specs) + [VMEM] * (len(args) - len(specs)),
        out_specs=jax.tree.map(lambda unused: VMEM, outs),
        scratch_shapes=list(scratch),
        cost_estimate=pl.CostEstimate(flops=0, bytes_accessed=0, transcendentals=0),
        compiler_params=pltpu.CompilerParams(vmem_limit_bytes=40 << 20),
    )(*args)


def split3(value):
    high = value.astype(BF16)
    rest = value - high.astype(F32)
    middle = rest.astype(BF16)
    low = (rest - middle.astype(F32)).astype(BF16)
    return high, middle, low


def over_columns(per_head):
    heads = per_head.shape[0]
    stacked = jnp.concatenate([part.astype(F32) for part in split3(per_head)], axis=0).astype(BF16)
    row = lax.broadcasted_iota(jnp.int32, (3 * heads, heads * HD), 0)
    column = lax.broadcasted_iota(jnp.int32, (3 * heads, heads * HD), 1)
    picks = (lax.rem(row, heads) == column // HD).astype(F32).astype(BF16)
    return lax.dot_general(stacked, picks, (((0,), (0,)), ((), ())), preferred_element_type=F32)


def decay_rows(per_head):
    wide = per_head
    high = wide.astype(BF16).astype(F32)
    return jnp.concatenate([high, wide - high], axis=1).astype(BF16)


def decays_of(rows):
    parts = rows.astype(F32)
    half = parts.shape[1] // 2
    total = parts[:, :half] + parts[:, half:]
    return jnp.concatenate([total, total], axis=1)


def block_kernel(
    where, grad_hbm, reads, log_decay, sums, cumulative, decays, one, two, three, grad, total, arrived
):
    fetches = (
        pltpu.make_async_copy(log_decay, total, arrived.at[0]),
        pltpu.make_async_copy(grad_hbm, grad, arrived.at[1]),
    )
    for fetch in fetches:
        fetch.start()
    heads, tokens = total.shape
    part = HD // QUAD
    fetches[0].wait()
    running = total[...]
    lane = lax.broadcasted_iota(jnp.int32, (heads, tokens), 1)
    step = 1
    while step < tokens:
        running = running + jnp.where(lane >= step, pltpu.roll(running, step, 1), 0.0)
        step *= 2
    cumulative[...] = running
    last = jnp.exp(running[:, tokens - 1 : tokens])
    decays[...] = jnp.broadcast_to(last, decays.shape)
    spread = over_columns(jnp.exp(running))
    fetches[1].wait()
    weighted = (spread * grad[...].astype(F32)).astype(BF16)
    sums[...] = lax.dot_general(
        weighted, reads[...], (((0,), (0,)), ((), ())), preferred_element_type=F32
    )
    rows = decay_rows(jnp.broadcast_to(last, (heads, decays.shape[1] // 2)))
    me = where[0]
    for flip, sent in ((1, one), (2, two), (3, three)):
        quarter = jnp.bitwise_xor(me, flip)
        for head in range(heads):
            start = pl.multiple_of(head * HD + quarter * part, part)
            sent[head * part : (head + 1) * part] = sums[pl.ds(start, part), :].astype(BF16)
        sent[heads * part :] = rows


def intra_kernel(
    where, skips, grad_hbm, conv_hbm, step_hbm, later_hbm, writes, reads, cumulative, after,
    fixed, slope, quarter, scores, steps, grad, conv_out, step_size, later, arrived,
):
    fetches = [
        pltpu.make_async_copy(source, target, arrived.at[place])
        for place, (source, target) in enumerate(
            ((step_hbm, step_size), (grad_hbm, grad), (conv_hbm, conv_out), (later_hbm, later))
        )
    ]
    for fetch in fetches:
        fetch.start()
    heads, tokens = cumulative.shape
    part = HD // QUAD
    half = tokens // 2
    scores[...] = lax.dot_general(
        writes[...], reads[...], (((1,), (1,)), ((), ())), preferred_element_type=F32
    )
    total = cumulative[...]
    columns = jnp.transpose(total)
    fetches[0].wait()
    steps[...] = over_columns(step_size[...])
    slope[...] = over_columns(
        step_size[...] * jnp.exp(total[:, tokens - 1 : tokens] - total)
    )
    causal = lax.broadcasted_iota(jnp.int32, (half, half), 1) >= lax.broadcasted_iota(
        jnp.int32, (half, half), 0
    )
    lane = lax.broadcasted_iota(jnp.int32, (half, 2 * HD), 1)
    for fetch in fetches[1:]:
        fetch.wait()
    for head in range(heads):
        start = pl.multiple_of(head * HD + where[0] * part, part)
        quarter[head] = later[pl.ds(start, part), :]
    for pair in range(heads // 2):
        span = slice(pair * 2 * HD, (pair + 1) * 2 * HD)
        skip = jnp.where(lane < HD, skips[2 * pair], skips[2 * pair + 1])
        for at in range(2):
            rows = slice(at * half, (at + 1) * half)
            both = []
            for head in (2 * pair, 2 * pair + 1):
                own = columns[rows, head : head + 1]
                offsets = total[head : head + 1, rows] - own
                mixing = (
                    jnp.exp(jnp.where(causal, offsets, -jnp.inf)) * scores[rows, rows]
                ).astype(BF16)
                sums = jnp.dot(mixing, grad[rows, span], preferred_element_type=F32)
                if at == 0:
                    rest = slice(half, tokens)
                    mixing = (
                        jnp.exp(total[head : head + 1, rest] - own) * scores[rows, rest]
                    ).astype(BF16)
                    sums = sums + jnp.dot(mixing, grad[rest, span], preferred_element_type=F32)
                both.append(sums)
            intra = jnp.where(lane < HD, both[0], both[1])
            activated = conv_out[rows, span].astype(F32)
            sigma = 1.0 / (1.0 + jnp.exp(-activated))
            gate = sigma * (1.0 + activated * (1.0 - sigma))
            fixed[rows, span] = gate * (
                steps[rows, span] * intra + skip * grad[rows, span].astype(F32)
            )
            slope[rows, span] = gate * slope[rows, span]


def gather_quad(me, sums, decays, received, values, scales):
    heads = decays.shape[0]
    part = HD // QUAD
    for head in range(heads):
        start = pl.multiple_of(head * HD + me * part, part)
        values[me, head] = sums[pl.ds(start, part), :]
    scales[me] = decays[...]
    for flip, came in enumerate(received, 1):
        other = jnp.bitwise_xor(me, flip)
        for head in range(heads):
            values[other, head] = came[head * part : (head + 1) * part].astype(F32)
        scales[other] = decays_of(came[heads * part :])


def quad_kernel(where, sums, decays, one, two, three, after, sent, values, scales):
    heads = decays.shape[0]
    part = HD // QUAD
    gather_quad(where[0], sums, decays, (one, two, three), values, scales)
    for head in range(heads):
        total = values[3, head]
        for block in (2, 1, 0):
            total = values[block, head] + scales[block][head : head + 1] * total
        sent[head * part : (head + 1) * part] = total.astype(BF16)
    product = scales[0] * scales[1] * scales[2] * scales[3]
    sent[heads * part :] = decay_rows(product[:, : product.shape[1] // 2])


def carry_kernel(
    where, sums, decays, one, two, three, middle, near, far, later, own, first, second, third,
    values, scales, carries,
):
    heads = decays.shape[0]
    part = HD // QUAD
    me, quad = where[0], where[1]
    gather_quad(me, sums, decays, (one, two, three), values, scales)
    jumps = []
    for ahead, came in ((3, far), (2, middle), (1, near)):
        present = jnp.full(decays.shape, quad + ahead, jnp.int32) < QUAD
        jumps.append((came, jnp.where(present, decays_of(came[heads * part :]), 1.0)))
    for head in range(heads):
        carry = later[head]
        for came, scale in jumps:
            sent = came[head * part : (head + 1) * part].astype(F32)
            carry = sent + scale[head : head + 1] * carry
        carries[3, head] = carry.astype(BF16)
        for block in (3, 2, 1):
            carry = values[block, head] + scales[block][head : head + 1] * carry
            carries[block - 1, head] = carry.astype(BF16)
    for flip, sent in ((0, own), (1, first), (2, second), (3, third)):
        sent[...] = carries[jnp.bitwise_xor(me, flip)]


def taps_sum(pre, taps, start, count):
    total = taps[0:1] * pre[start : start + count]
    for tap in range(1, KW):
        total = total + taps[tap : tap + 1] * pre[start + tap : start + tap + count]
    return total.astype(BF16)


def join_kernel(
    where, own, first, second, third, writes, fixed, slope, taps, chunk, rim, rest, carried, pre
):
    heads = own.shape[0]
    part = HD // QUAD
    me = where[0]
    for flip, came in ((0, own), (1, first), (2, second), (3, third)):
        quarter = jnp.bitwise_xor(me, flip)
        for head in range(heads):
            spot = pl.ds(pl.multiple_of(head * HD + quarter * part, part), part)
            carried[spot, :] = came[head]
    count = chunk.shape[0]
    inter = lax.dot_general(
        writes[...], carried[...], (((1,), (1,)), ((), ())), preferred_element_type=F32
    )
    rounded = (fixed[...] + slope[...] * inter).astype(BF16)
    rim[...] = rounded[:16]
    rest[...] = rounded[count:]
    pre[...] = rounded[: count + 16].astype(F32)
    chunk[...] = taps_sum(pre, taps, 0, count)


def tail_kernel(rest, rim, taps, chunk, pre):
    count = rest.shape[0]
    pre[:count] = rest[...].astype(F32)
    pre[count:] = rim[...].astype(F32)
    chunk[...] = taps_sum(pre, taps, 0, count)


def output_kernel(sums, decays, carried, head, last, after, state, x_grad):
    for at in range(decays.shape[0]):
        spot = slice(at * HD, (at + 1) * HD)
        state[spot] = sums[spot] + decays[at : at + 1] * carried[spot].astype(F32)
    x_grad[: head.shape[0]] = head[...]
    x_grad[head.shape[0] :] = last[...]


def product_kernel(where, own, far, near, weight, after, total):
    column = where[3]
    width = own.shape[1]
    for place in range(4):
        spot = slice(place * width, (place + 1) * width)
        sums = None
        for flip, piece in ((0, own), (1, near), (3, far)):
            source = jnp.bitwise_xor(column, flip)
            at = pl.ds(pl.multiple_of(source * width, width), width)
            term = lax.dot_general(
                piece[...], weight[spot, at], (((1,), (1,)), ((), ())), preferred_element_type=F32
            )
            sums = term if sums is None else sums + term
        total[:, spot] = sums


def finish_kernel(flips, where, across, weight, total, *outs):
    row, column = where[2], where[3]
    width = across.shape[1]
    at = pl.ds(pl.multiple_of(jnp.bitwise_xor(column, 2) * width, width), width)
    for flip, out in zip(flips, outs):
        target = jnp.bitwise_xor(row, flip)
        spot = pl.ds(pl.multiple_of(target * width, width), width)
        term = lax.dot_general(
            across[...], weight[spot, at], (((1,), (1,)), ((), ())), preferred_element_type=F32
        )
        out[...] = (total[:, spot] + term).astype(out.dtype)


def earlier(value, steps):
    count = lax.axis_size("ctx")
    return lax.ppermute(value, "ctx", [(place, place - steps) for place in range(steps, count)])


def swapped(value, axis, flip):
    count = lax.axis_size(axis)
    return lax.ppermute(value, axis, [(place, place ^ flip) for place in range(count)])


def on_device(
    output_grad, conv_out, input_mix, output_mix, step_size, log_decay, skip_gain, conv_weight,
    later_grad, proj_weight,
):
    tokens, width = output_grad.shape
    heads = step_size.shape[0]
    states = input_mix.shape[2]
    part = HD // QUAD
    ctx, row, column = lax.axis_index("ctx"), lax.axis_index("row"), lax.axis_index("col")
    where = jnp.stack([ctx % QUAD, ctx // QUAD, row, column]).astype(jnp.int32)
    group = (row * lax.axis_size("col") + column) * heads // HPG
    reads = lax.dynamic_index_in_dim(output_mix, group, 1, keepdims=False)
    writes = lax.dynamic_index_in_dim(input_mix, group, 1, keepdims=False)
    later = later_grad.reshape(width, states)

    message = struct((heads * part + heads, states), BF16)
    piece = struct((heads, part, states), BF16)
    wide = struct((width, states), F32)
    plane = struct((tokens, width), F32)
    sums, cumulative, decays, *out = call(
        block_kernel,
        (wide, struct((heads, tokens), F32), struct((heads, states), F32)) + (message,) * 3,
        (where, output_grad, reads, log_decay),
        specs=(SMEM, HBM, VMEM, HBM),
        scratch=(
            pltpu.VMEM((tokens, width), BF16),
            pltpu.VMEM((heads, tokens), F32),
            pltpu.SemaphoreType.DMA((2,)),
        ),
    )
    near = [swapped(value, "ctx", flip) for flip, value in enumerate(out, 1)]
    quads = (
        pltpu.VMEM((QUAD, heads, part, states), F32),
        pltpu.VMEM((QUAD, heads, states), F32),
    )
    joined = call(
        quad_kernel, message, (where, sums, decays, *near, writes), specs=(SMEM,), scratch=quads,
    )
    far, middle, close = (earlier(joined, QUAD * ahead) for ahead in (3, 2, 1))
    fixed, slope, quarter = call(
        intra_kernel,
        (plane, plane, struct((heads, part, states), F32)),
        (where, skip_gain, output_grad, conv_out, step_size, later, writes, reads, cumulative)
        + (joined,),
        specs=(SMEM, SMEM, HBM, HBM, HBM, HBM),
        scratch=(
            pltpu.VMEM((tokens, tokens), F32),
            pltpu.VMEM((tokens, width), F32),
            pltpu.VMEM((tokens, width), BF16),
            pltpu.VMEM((tokens, width), BF16),
            pltpu.VMEM((heads, tokens), F32),
            pltpu.VMEM((width, states), F32),
            pltpu.SemaphoreType.DMA((4,)),
        ),
    )
    own, *out = call(
        carry_kernel,
        (piece,) * 4,
        (where, sums, decays, *near, middle, close, far, quarter),
        specs=(SMEM,),
        scratch=quads + (pltpu.VMEM((QUAD, heads, part, states), BF16),),
    )
    parts = [swapped(value, "ctx", flip) for flip, value in enumerate(out, 1)]
    blocks = [struct((count, width), BF16) for count in (FIRST, tokens - FIRST)]
    head, rim, rest, carried = call(
        join_kernel,
        (blocks[0], struct((16, width), BF16), blocks[1], struct((width, states), BF16)),
        (where, own, *parts, writes, fixed, slope, conv_weight),
        specs=(SMEM,),
        scratch=(pltpu.VMEM((FIRST + 16, width), F32),),
    )
    last = call(
        tail_kernel,
        blocks[1],
        (rest, earlier(rim, 1), conv_weight),
        scratch=(pltpu.VMEM((tokens - FIRST + 16, width), F32),),
    )
    sums_of, after = [], head
    for chunk in (head, last):
        near, far, across = (swapped(chunk, "col", flip) for flip in (1, 3, 2))
        block, held = struct(chunk.shape, BF16), struct(chunk.shape, F32)
        partial = call(
            product_kernel,
            struct((chunk.shape[0], proj_weight.shape[0]), F32),
            (where, chunk, far, near, proj_weight, after),
            specs=(SMEM,),
        )
        near, far = call(
            functools.partial(finish_kernel, (1, 3)),
            (block, block),
            (where, across, proj_weight, partial),
            specs=(SMEM,),
        )
        over, kept = call(
            functools.partial(finish_kernel, (2, 0)),
            (block, held),
            (where, across, proj_weight, partial),
            specs=(SMEM,),
        )
        came = [swapped(value, "row", flip) for value, flip in ((near, 1), (far, 3), (over, 2))]
        sums_of.append((kept, *came))
        after = kept
    state, x_grad = call(
        output_kernel,
        (wide, struct((tokens, width), BF16)),
        (sums, decays, carried, head, last, came[0]),
    )
    kept, *came = sums_of[-1]
    sums_of[-1] = lax.optimization_barrier((kept, *came, state))[:-1]
    sums_of = [kept + sum(value.astype(F32) for value in came) for kept, *came in sums_of]
    hidden_grad = jnp.concatenate(sums_of, axis=0).astype(BF16)
    return hidden_grad, x_grad, state.reshape(1, heads, HD, states)


def solution(mesh):
    return jax.shard_map(
        on_device,
        mesh=mesh,
        in_specs=(
            P("ctx", ("row", "col")),
            P("ctx", ("row", "col")),
            P("ctx", None, None),
            P("ctx", None, None),
            P(("row", "col"), "ctx"),
            P(("row", "col"), "ctx"),
            P(("row", "col")),
            P(None, ("row", "col")),
            P(("row", "col"), None, None),
            P("col", "row"),
        ),
        out_specs=(
            P("ctx", ("col", "row")),
            P("ctx", ("row", "col")),
            P("ctx", ("row", "col"), None, None),
        ),
        check_vma=False,
    )
```

```python
import functools

import jax
import jax.numpy as jnp
from jax import lax
from jax.experimental import pallas as pl
from jax.experimental.pallas import tpu as pltpu
from jax.sharding import PartitionSpec as P

HD = 64
HPG = 32
KW = 4
QUAD = 4
F32 = jnp.float32
BF16 = jnp.bfloat16
VMEM = pl.BlockSpec(memory_space=pltpu.VMEM)
SMEM = pl.BlockSpec(memory_space=pltpu.SMEM)
HBM = pl.BlockSpec(memory_space=pltpu.HBM)
FIRST = 256


def struct(shape, dtype):
    return jax.ShapeDtypeStruct(shape, dtype)


def call(kernel, outs, args, specs=(), scratch=()):
    return pl.pallas_call(
        kernel,
        out_shape=outs,
        in_specs=list(specs) + [VMEM] * (len(args) - len(specs)),
        out_specs=jax.tree.map(lambda unused: VMEM, outs),
        scratch_shapes=list(scratch),
        cost_estimate=pl.CostEstimate(flops=0, bytes_accessed=0, transcendentals=0),
        compiler_params=pltpu.CompilerParams(vmem_limit_bytes=40 << 20),
    )(*args)


def split3(value):
    high = value.astype(BF16)
    rest = value - high.astype(F32)
    middle = rest.astype(BF16)
    low = (rest - middle.astype(F32)).astype(BF16)
    return high, middle, low


def over_columns(per_head):
    heads = per_head.shape[0]
    stacked = jnp.concatenate([part.astype(F32) for part in split3(per_head)], axis=0).astype(BF16)
    row = lax.broadcasted_iota(jnp.int32, (3 * heads, heads * HD), 0)
    column = lax.broadcasted_iota(jnp.int32, (3 * heads, heads * HD), 1)
    picks = (lax.rem(row, heads) == column // HD).astype(F32).astype(BF16)
    return lax.dot_general(stacked, picks, (((0,), (0,)), ((), ())), preferred_element_type=F32)


def decay_rows(per_head):
    wide = per_head
    high = wide.astype(BF16).astype(F32)
    return jnp.concatenate([high, wide - high], axis=1).astype(BF16)


def decays_of(rows):
    parts = rows.astype(F32)
    half = parts.shape[1] // 2
    total = parts[:, :half] + parts[:, half:]
    return jnp.concatenate([total, total], axis=1)


def block_kernel(
    where, grad_hbm, reads, log_decay, sums, cumulative, decays, one, two, three, grad, total, arrived
):
    fetches = (
        pltpu.make_async_copy(log_decay, total, arrived.at[0]),
        pltpu.make_async_copy(grad_hbm, grad, arrived.at[1]),
    )
    for fetch in fetches:
        fetch.start()
    heads, tokens = total.shape
    part = HD // QUAD
    fetches[0].wait()
    running = total[...]
    lane = lax.broadcasted_iota(jnp.int32, (heads, tokens), 1)
    step = 1
    while step < tokens:
        running = running + jnp.where(lane >= step, pltpu.roll(running, step, 1), 0.0)
        step *= 2
    cumulative[...] = running
    last = jnp.exp(running[:, tokens - 1 : tokens])
    decays[...] = jnp.broadcast_to(last, decays.shape)
    spread = over_columns(jnp.exp(running))
    fetches[1].wait()
    weighted = (spread * grad[...].astype(F32)).astype(BF16)
    sums[...] = lax.dot_general(
        weighted, reads[...], (((0,), (0,)), ((), ())), preferred_element_type=F32
    )
    rows = decay_rows(jnp.broadcast_to(last, (heads, decays.shape[1] // 2)))
    me = where[0]
    for flip, sent in ((1, one), (2, two), (3, three)):
        quarter = jnp.bitwise_xor(me, flip)
        for head in range(heads):
            start = pl.multiple_of(head * HD + quarter * part, part)
            sent[head * part : (head + 1) * part] = sums[pl.ds(start, part), :].astype(BF16)
        sent[heads * part :] = rows


def intra_kernel(
    where, skips, grad_hbm, conv_hbm, step_hbm, later_hbm, writes, reads, cumulative, after,
    fixed, slope, quarter, scores, steps, grad, conv_out, step_size, later, arrived,
):
    fetches = [
        pltpu.make_async_copy(source, target, arrived.at[place])
        for place, (source, target) in enumerate(
            ((step_hbm, step_size), (grad_hbm, grad), (conv_hbm, conv_out), (later_hbm, later))
        )
    ]
    for fetch in fetches:
        fetch.start()
    heads, tokens = cumulative.shape
    part = HD // QUAD
    half = tokens // 2
    scores[...] = lax.dot_general(
        writes[...], reads[...], (((1,), (1,)), ((), ())), preferred_element_type=F32
    )
    total = cumulative[...]
    columns = jnp.transpose(total)
    fetches[0].wait()
    steps[...] = over_columns(step_size[...])
    slope[...] = over_columns(
        step_size[...] * jnp.exp(total[:, tokens - 1 : tokens] - total)
    )
    causal = lax.broadcasted_iota(jnp.int32, (half, half), 1) >= lax.broadcasted_iota(
        jnp.int32, (half, half), 0
    )
    lane = lax.broadcasted_iota(jnp.int32, (half, 2 * HD), 1)
    for fetch in fetches[1:]:
        fetch.wait()
    for head in range(heads):
        start = pl.multiple_of(head * HD + where[0] * part, part)
        quarter[head] = later[pl.ds(start, part), :]
    for pair in range(heads // 2):
        span = slice(pair * 2 * HD, (pair + 1) * 2 * HD)
        skip = jnp.where(lane < HD, skips[2 * pair], skips[2 * pair + 1])
        for at in range(2):
            rows = slice(at * half, (at + 1) * half)
            both = []
            for head in (2 * pair, 2 * pair + 1):
                own = columns[rows, head : head + 1]
                offsets = total[head : head + 1, rows] - own
                mixing = (
                    jnp.exp(jnp.where(causal, offsets, -jnp.inf)) * scores[rows, rows]
                ).astype(BF16)
                sums = jnp.dot(mixing, grad[rows, span], preferred_element_type=F32)
                if at == 0:
                    rest = slice(half, tokens)
                    mixing = (
                        jnp.exp(total[head : head + 1, rest] - own) * scores[rows, rest]
                    ).astype(BF16)
                    sums = sums + jnp.dot(mixing, grad[rest, span], preferred_element_type=F32)
                both.append(sums)
            intra = jnp.where(lane < HD, both[0], both[1])
            activated = conv_out[rows, span].astype(F32)
            sigma = 1.0 / (1.0 + jnp.exp(-activated))
            gate = sigma * (1.0 + activated * (1.0 - sigma))
            fixed[rows, span] = gate * (
                steps[rows, span] * intra + skip * grad[rows, span].astype(F32)
            )
            slope[rows, span] = gate * slope[rows, span]


def gather_quad(me, sums, decays, received, values, scales):
    heads = decays.shape[0]
    part = HD // QUAD
    for head in range(heads):
        start = pl.multiple_of(head * HD + me * part, part)
        values[me, head] = sums[pl.ds(start, part), :]
    scales[me] = decays[...]
    for flip, came in enumerate(received, 1):
        other = jnp.bitwise_xor(me, flip)
        for head in range(heads):
            values[other, head] = came[head * part : (head + 1) * part].astype(F32)
        scales[other] = decays_of(came[heads * part :])


def quad_kernel(where, sums, decays, one, two, three, after, sent, values, scales):
    heads = decays.shape[0]
    part = HD // QUAD
    gather_quad(where[0], sums, decays, (one, two, three), values, scales)
    for head in range(heads):
        total = values[3, head]
        for block in (2, 1, 0):
            total = values[block, head] + scales[block][head : head + 1] * total
        sent[head * part : (head + 1) * part] = total.astype(BF16)
    product = scales[0] * scales[1] * scales[2] * scales[3]
    sent[heads * part :] = decay_rows(product[:, : product.shape[1] // 2])


def carry_kernel(
    where, sums, decays, one, two, three, middle, near, far, later, own, first, second, third,
    values, scales, carries,
):
    heads = decays.shape[0]
    part = HD // QUAD
    me, quad = where[0], where[1]
    gather_quad(me, sums, decays, (one, two, three), values, scales)
    jumps = []
    for ahead, came in ((3, far), (2, middle), (1, near)):
        present = jnp.full(decays.shape, quad + ahead, jnp.int32) < QUAD
        jumps.append((came, jnp.where(present, decays_of(came[heads * part :]), 1.0)))
    for head in range(heads):
        carry = later[head]
        for came, scale in jumps:
            sent = came[head * part : (head + 1) * part].astype(F32)
            carry = sent + scale[head : head + 1] * carry
        carries[3, head] = carry.astype(BF16)
        for block in (3, 2, 1):
            carry = values[block, head] + scales[block][head : head + 1] * carry
            carries[block - 1, head] = carry.astype(BF16)
    for flip, sent in ((0, own), (1, first), (2, second), (3, third)):
        sent[...] = carries[jnp.bitwise_xor(me, flip)]


def taps_sum(pre, taps, start, count):
    total = taps[0:1] * pre[start : start + count]
    for tap in range(1, KW):
        total = total + taps[tap : tap + 1] * pre[start + tap : start + tap + count]
    return total.astype(BF16)


def join_kernel(
    where, own, first, second, third, writes, fixed, slope, taps, chunk, rim, rest, carried, pre
):
    heads = own.shape[0]
    part = HD // QUAD
    me = where[0]
    for flip, came in ((0, own), (1, first), (2, second), (3, third)):
        quarter = jnp.bitwise_xor(me, flip)
        for head in range(heads):
            spot = pl.ds(pl.multiple_of(head * HD + quarter * part, part), part)
            carried[spot, :] = came[head]
    count = chunk.shape[0]
    inter = lax.dot_general(
        writes[...], carried[...], (((1,), (1,)), ((), ())), preferred_element_type=F32
    )
    rounded = (fixed[...] + slope[...] * inter).astype(BF16)
    rim[...] = rounded[:16]
    rest[...] = rounded[count:]
    pre[...] = rounded[: count + 16].astype(F32)
    chunk[...] = taps_sum(pre, taps, 0, count)


def tail_kernel(rest, rim, taps, chunk, pre):
    count = rest.shape[0]
    pre[:count] = rest[...].astype(F32)
    pre[count:] = rim[...].astype(F32)
    chunk[...] = taps_sum(pre, taps, 0, count)


def output_kernel(sums, decays, carried, head, last, after, state, x_grad):
    for at in range(decays.shape[0]):
        spot = slice(at * HD, (at + 1) * HD)
        state[spot] = sums[spot] + decays[at : at + 1] * carried[spot].astype(F32)
    x_grad[: head.shape[0]] = head[...]
    x_grad[head.shape[0] :] = last[...]


def product_kernel(where, own, far, near, weight, after, total):
    column = where[3]
    width = own.shape[1]
    for place in range(4):
        spot = slice(place * width, (place + 1) * width)
        sums = None
        for flip, piece in ((0, own), (1, near), (3, far)):
            source = jnp.bitwise_xor(column, flip)
            at = pl.ds(pl.multiple_of(source * width, width), width)
            term = lax.dot_general(
                piece[...], weight[spot, at], (((1,), (1,)), ((), ())), preferred_element_type=F32
            )
            sums = term if sums is None else sums + term
        total[:, spot] = sums


def finish_kernel(flips, where, across, weight, total, *outs):
    row, column = where[2], where[3]
    width = across.shape[1]
    at = pl.ds(pl.multiple_of(jnp.bitwise_xor(column, 2) * width, width), width)
    for flip, out in zip(flips, outs):
        target = jnp.bitwise_xor(row, flip)
        spot = pl.ds(pl.multiple_of(target * width, width), width)
        term = lax.dot_general(
            across[...], weight[spot, at], (((1,), (1,)), ((), ())), preferred_element_type=F32
        )
        out[...] = (total[:, spot] + term).astype(out.dtype)


def earlier(value, steps):
    count = lax.axis_size("ctx")
    return lax.ppermute(value, "ctx", [(place, place - steps) for place in range(steps, count)])


def swapped(value, axis, flip):
    count = lax.axis_size(axis)
    return lax.ppermute(value, axis, [(place, place ^ flip) for place in range(count)])


def on_device(
    output_grad, conv_out, input_mix, output_mix, step_size, log_decay, skip_gain, conv_weight,
    later_grad, proj_weight,
):
    tokens, width = output_grad.shape
    heads = step_size.shape[0]
    states = input_mix.shape[2]
    part = HD // QUAD
    ctx, row, column = lax.axis_index("ctx"), lax.axis_index("row"), lax.axis_index("col")
    where = jnp.stack([ctx % QUAD, ctx // QUAD, row, column]).astype(jnp.int32)
    group = (row * lax.axis_size("col") + column) * heads // HPG
    reads = lax.dynamic_index_in_dim(output_mix, group, 1, keepdims=False)
    writes = lax.dynamic_index_in_dim(input_mix, group, 1, keepdims=False)
    later = later_grad.reshape(width, states)

    message = struct((heads * part + heads, states), BF16)
    piece = struct((heads, part, states), BF16)
    wide = struct((width, states), F32)
    plane = struct((tokens, width), F32)
    sums, cumulative, decays, *out = call(
        block_kernel,
        (wide, struct((heads, tokens), F32), struct((heads, states), F32)) + (message,) * 3,
        (where, output_grad, reads, log_decay),
        specs=(SMEM, HBM, VMEM, HBM),
        scratch=(
            pltpu.VMEM((tokens, width), BF16),
            pltpu.VMEM((heads, tokens), F32),
            pltpu.SemaphoreType.DMA((2,)),
        ),
    )
    near = [swapped(value, "ctx", flip) for flip, value in enumerate(out, 1)]
    quads = (
        pltpu.VMEM((QUAD, heads, part, states), F32),
        pltpu.VMEM((QUAD, heads, states), F32),
    )
    joined = call(
        quad_kernel, message, (where, sums, decays, *near, writes), specs=(SMEM,), scratch=quads,
    )
    far, middle, close = (earlier(joined, QUAD * ahead) for ahead in (3, 2, 1))
    fixed, slope, quarter = call(
        intra_kernel,
        (plane, plane, struct((heads, part, states), F32)),
        (where, skip_gain, output_grad, conv_out, step_size, later, writes, reads, cumulative)
        + (joined,),
        specs=(SMEM, SMEM, HBM, HBM, HBM, HBM),
        scratch=(
            pltpu.VMEM((tokens, tokens), F32),
            pltpu.VMEM((tokens, width), F32),
            pltpu.VMEM((tokens, width), BF16),
            pltpu.VMEM((tokens, width), BF16),
            pltpu.VMEM((heads, tokens), F32),
            pltpu.VMEM((width, states), F32),
            pltpu.SemaphoreType.DMA((4,)),
        ),
    )
    own, *out = call(
        carry_kernel,
        (piece,) * 4,
        (where, sums, decays, *near, middle, close, far, quarter),
        specs=(SMEM,),
        scratch=quads + (pltpu.VMEM((QUAD, heads, part, states), BF16),),
    )
    parts = [swapped(value, "ctx", flip) for flip, value in enumerate(out, 1)]
    blocks = [struct((count, width), BF16) for count in (FIRST, tokens - FIRST)]
    head, rim, rest, carried = call(
        join_kernel,
        (blocks[0], struct((16, width), BF16), blocks[1], struct((width, states), BF16)),
        (where, own, *parts, writes, fixed, slope, conv_weight),
        specs=(SMEM,),
        scratch=(pltpu.VMEM((FIRST + 16, width), F32),),
    )
    last = call(
        tail_kernel,
        blocks[1],
        (rest, earlier(rim, 1), conv_weight),
        scratch=(pltpu.VMEM((tokens - FIRST + 16, width), F32),),
    )
    sums_of, after = [], head
    for chunk in (head, last):
        near, far, across = (swapped(chunk, "col", flip) for flip in (1, 3, 2))
        block, held = struct(chunk.shape, BF16), struct(chunk.shape, F32)
        partial = call(
            product_kernel,
            struct((chunk.shape[0], proj_weight.shape[0]), F32),
            (where, chunk, far, near, proj_weight, after),
            specs=(SMEM,),
        )
        near, far = call(
            functools.partial(finish_kernel, (1, 3)),
            (block, block),
            (where, across, proj_weight, partial),
            specs=(SMEM,),
        )
        over, kept = call(
            functools.partial(finish_kernel, (2, 0)),
            (block, held),
            (where, across, proj_weight, partial),
            specs=(SMEM,),
        )
        came = [swapped(value, "row", flip) for value, flip in ((far, 3), (near, 1), (over, 2))]
        sums_of.append((kept, *came))
        after = kept
    state, x_grad = call(
        output_kernel,
        (wide, struct((tokens, width), BF16)),
        (sums, decays, carried, head, last, came[0]),
    )
    kept, *came = sums_of[-1]
    sums_of[-1] = lax.optimization_barrier((kept, *came, state))[:-1]
    sums_of = [kept + sum(value.astype(F32) for value in came) for kept, *came in sums_of]
    hidden_grad = jnp.concatenate(sums_of, axis=0).astype(BF16)
    return hidden_grad, x_grad, state.reshape(1, heads, HD, states)


def solution(mesh):
    return jax.shard_map(
        on_device,
        mesh=mesh,
        in_specs=(
            P("ctx", ("row", "col")),
            P("ctx", ("row", "col")),
            P("ctx", None, None),
            P("ctx", None, None),
            P(("row", "col"), "ctx"),
            P(("row", "col"), "ctx"),
            P(("row", "col")),
            P(None, ("row", "col")),
            P(("row", "col"), None, None),
            P("col", "row"),
        ),
        out_specs=(
            P("ctx", ("col", "row")),
            P("ctx", ("row", "col")),
            P("ctx", ("row", "col"), None, None),
        ),
        check_vma=False,
    )
```

```python
import functools

import jax
import jax.numpy as jnp
from jax import lax
from jax.experimental import pallas as pl
from jax.experimental.pallas import tpu as pltpu
from jax.sharding import PartitionSpec as P

HD = 64
HPG = 32
KW = 4
QUAD = 4
F32 = jnp.float32
BF16 = jnp.bfloat16
VMEM = pl.BlockSpec(memory_space=pltpu.VMEM)
SMEM = pl.BlockSpec(memory_space=pltpu.SMEM)
HBM = pl.BlockSpec(memory_space=pltpu.HBM)
FIRST = 256


def struct(shape, dtype):
    return jax.ShapeDtypeStruct(shape, dtype)


def call(kernel, outs, args, specs=(), scratch=()):
    return pl.pallas_call(
        kernel,
        out_shape=outs,
        in_specs=list(specs) + [VMEM] * (len(args) - len(specs)),
        out_specs=jax.tree.map(lambda unused: VMEM, outs),
        scratch_shapes=list(scratch),
        cost_estimate=pl.CostEstimate(flops=0, bytes_accessed=0, transcendentals=0),
        compiler_params=pltpu.CompilerParams(vmem_limit_bytes=40 << 20),
    )(*args)


def split3(value):
    high = value.astype(BF16)
    rest = value - high.astype(F32)
    middle = rest.astype(BF16)
    low = (rest - middle.astype(F32)).astype(BF16)
    return high, middle, low


def over_columns(per_head):
    heads = per_head.shape[0]
    stacked = jnp.concatenate([part.astype(F32) for part in split3(per_head)], axis=0).astype(BF16)
    row = lax.broadcasted_iota(jnp.int32, (3 * heads, heads * HD), 0)
    column = lax.broadcasted_iota(jnp.int32, (3 * heads, heads * HD), 1)
    picks = (lax.rem(row, heads) == column // HD).astype(F32).astype(BF16)
    return lax.dot_general(stacked, picks, (((0,), (0,)), ((), ())), preferred_element_type=F32)


def decay_rows(per_head):
    wide = per_head
    high = wide.astype(BF16).astype(F32)
    return jnp.concatenate([high, wide - high], axis=1).astype(BF16)


def decays_of(rows):
    parts = rows.astype(F32)
    half = parts.shape[1] // 2
    total = parts[:, :half] + parts[:, half:]
    return jnp.concatenate([total, total], axis=1)


def block_kernel(
    where, grad_hbm, reads, log_decay, sums, cumulative, decays, one, two, three, grad, total, arrived
):
    fetches = (
        pltpu.make_async_copy(log_decay, total, arrived.at[0]),
        pltpu.make_async_copy(grad_hbm, grad, arrived.at[1]),
    )
    for fetch in fetches:
        fetch.start()
    heads, tokens = total.shape
    part = HD // QUAD
    fetches[0].wait()
    running = total[...]
    lane = lax.broadcasted_iota(jnp.int32, (heads, tokens), 1)
    step = 1
    while step < tokens:
        running = running + jnp.where(lane >= step, pltpu.roll(running, step, 1), 0.0)
        step *= 2
    cumulative[...] = running
    last = jnp.exp(running[:, tokens - 1 : tokens])
    decays[...] = jnp.broadcast_to(last, decays.shape)
    spread = over_columns(jnp.exp(running))
    fetches[1].wait()
    weighted = (spread * grad[...].astype(F32)).astype(BF16)
    sums[...] = lax.dot_general(
        weighted, reads[...], (((0,), (0,)), ((), ())), preferred_element_type=F32
    )
    rows = decay_rows(jnp.broadcast_to(last, (heads, decays.shape[1] // 2)))
    me = where[0]
    for flip, sent in ((1, one), (2, two), (3, three)):
        quarter = jnp.bitwise_xor(me, flip)
        for head in range(heads):
            start = pl.multiple_of(head * HD + quarter * part, part)
            sent[head * part : (head + 1) * part] = sums[pl.ds(start, part), :].astype(BF16)
        sent[heads * part :] = rows


def intra_kernel(
    where, skips, grad_hbm, conv_hbm, step_hbm, later_hbm, writes, reads, cumulative, after,
    fixed, slope, quarter, scores, steps, grad, conv_out, step_size, later, arrived,
):
    fetches = [
        pltpu.make_async_copy(source, target, arrived.at[place])
        for place, (source, target) in enumerate(
            ((step_hbm, step_size), (grad_hbm, grad), (conv_hbm, conv_out), (later_hbm, later))
        )
    ]
    for fetch in fetches:
        fetch.start()
    heads, tokens = cumulative.shape
    part = HD // QUAD
    half = tokens // 2
    scores[...] = lax.dot_general(
        writes[...], reads[...], (((1,), (1,)), ((), ())), preferred_element_type=F32
    )
    total = cumulative[...]
    columns = jnp.transpose(total)
    fetches[0].wait()
    steps[...] = over_columns(step_size[...])
    slope[...] = over_columns(
        step_size[...] * jnp.exp(total[:, tokens - 1 : tokens] - total)
    )
    causal = lax.broadcasted_iota(jnp.int32, (half, half), 1) >= lax.broadcasted_iota(
        jnp.int32, (half, half), 0
    )
    lane = lax.broadcasted_iota(jnp.int32, (half, 2 * HD), 1)
    for fetch in fetches[1:]:
        fetch.wait()
    for head in range(heads):
        start = pl.multiple_of(head * HD + where[0] * part, part)
        quarter[head] = later[pl.ds(start, part), :]
    for pair in range(heads // 2):
        span = slice(pair * 2 * HD, (pair + 1) * 2 * HD)
        skip = jnp.where(lane < HD, skips[2 * pair], skips[2 * pair + 1])
        for at in range(2):
            rows = slice(at * half, (at + 1) * half)
            both = []
            for head in (2 * pair, 2 * pair + 1):
                own = columns[rows, head : head + 1]
                offsets = total[head : head + 1, rows] - own
                mixing = (
                    jnp.exp(jnp.where(causal, offsets, -jnp.inf)) * scores[rows, rows]
                ).astype(BF16)
                sums = jnp.dot(mixing, grad[rows, span], preferred_element_type=F32)
                if at == 0:
                    rest = slice(half, tokens)
                    mixing = (
                        jnp.exp(total[head : head + 1, rest] - own) * scores[rows, rest]
                    ).astype(BF16)
                    sums = sums + jnp.dot(mixing, grad[rest, span], preferred_element_type=F32)
                both.append(sums)
            intra = jnp.where(lane < HD, both[0], both[1])
            activated = conv_out[rows, span].astype(F32)
            sigma = 1.0 / (1.0 + jnp.exp(-activated))
            gate = sigma * (1.0 + activated * (1.0 - sigma))
            fixed[rows, span] = gate * (
                steps[rows, span] * intra + skip * grad[rows, span].astype(F32)
            )
            slope[rows, span] = gate * slope[rows, span]


def gather_quad(me, sums, decays, received, values, scales):
    heads = decays.shape[0]
    part = HD // QUAD
    for head in range(heads):
        start = pl.multiple_of(head * HD + me * part, part)
        values[me, head] = sums[pl.ds(start, part), :]
    scales[me] = decays[...]
    for flip, came in enumerate(received, 1):
        other = jnp.bitwise_xor(me, flip)
        for head in range(heads):
            values[other, head] = came[head * part : (head + 1) * part].astype(F32)
        scales[other] = decays_of(came[heads * part :])


def quad_kernel(where, sums, decays, one, two, three, after, sent, values, scales):
    heads = decays.shape[0]
    part = HD // QUAD
    gather_quad(where[0], sums, decays, (one, two, three), values, scales)
    for head in range(heads):
        total = values[3, head]
        for block in (2, 1, 0):
            total = values[block, head] + scales[block][head : head + 1] * total
        sent[head * part : (head + 1) * part] = total.astype(BF16)
    product = scales[0] * scales[1] * scales[2] * scales[3]
    sent[heads * part :] = decay_rows(product[:, : product.shape[1] // 2])


def carry_kernel(
    where, sums, decays, one, two, three, middle, near, far, later, own, first, second, third,
    values, scales, carries,
):
    heads = decays.shape[0]
    part = HD // QUAD
    me, quad = where[0], where[1]
    gather_quad(me, sums, decays, (one, two, three), values, scales)
    jumps = []
    for ahead, came in ((3, far), (2, middle), (1, near)):
        present = jnp.full(decays.shape, quad + ahead, jnp.int32) < QUAD
        jumps.append((came, jnp.where(present, decays_of(came[heads * part :]), 1.0)))
    for head in range(heads):
        carry = later[head]
        for came, scale in jumps:
            sent = came[head * part : (head + 1) * part].astype(F32)
            carry = sent + scale[head : head + 1] * carry
        carries[3, head] = carry.astype(BF16)
        for block in (3, 2, 1):
            carry = values[block, head] + scales[block][head : head + 1] * carry
            carries[block - 1, head] = carry.astype(BF16)
    for flip, sent in ((0, own), (1, first), (2, second), (3, third)):
        sent[...] = carries[jnp.bitwise_xor(me, flip)]


def taps_sum(pre, taps, start, count):
    total = taps[0:1] * pre[start : start + count]
    for tap in range(1, KW):
        total = total + taps[tap : tap + 1] * pre[start + tap : start + tap + count]
    return total.astype(BF16)


def join_kernel(
    where, own, first, second, third, writes, fixed, slope, taps, chunk, rim, rest, carried, pre
):
    heads = own.shape[0]
    part = HD // QUAD
    me = where[0]
    for flip, came in ((0, own), (1, first), (2, second), (3, third)):
        quarter = jnp.bitwise_xor(me, flip)
        for head in range(heads):
            spot = pl.ds(pl.multiple_of(head * HD + quarter * part, part), part)
            carried[spot, :] = came[head]
    count = chunk.shape[0]
    inter = lax.dot_general(
        writes[...], carried[...], (((1,), (1,)), ((), ())), preferred_element_type=F32
    )
    rounded = (fixed[...] + slope[...] * inter).astype(BF16)
    rim[...] = rounded[:8]
    rest[...] = rounded[count:]
    pre[...] = rounded[: count + 16].astype(F32)
    chunk[...] = taps_sum(pre, taps, 0, count)


def tail_kernel(rest, rim, taps, chunk, pre):
    count = rest.shape[0]
    pre[:count] = rest[...].astype(F32)
    pre[count:] = rim[...].astype(F32)
    chunk[...] = taps_sum(pre, taps, 0, count)


def output_kernel(sums, decays, carried, head, last, after, state, x_grad):
    for at in range(decays.shape[0]):
        spot = slice(at * HD, (at + 1) * HD)
        state[spot] = sums[spot] + decays[at : at + 1] * carried[spot].astype(F32)
    x_grad[: head.shape[0]] = head[...]
    x_grad[head.shape[0] :] = last[...]


def product_kernel(where, own, far, near, weight, after, total):
    column = where[3]
    width = own.shape[1]
    for place in range(4):
        spot = slice(place * width, (place + 1) * width)
        sums = None
        for flip, piece in ((0, own), (1, near), (3, far)):
            source = jnp.bitwise_xor(column, flip)
            at = pl.ds(pl.multiple_of(source * width, width), width)
            term = lax.dot_general(
                piece[...], weight[spot, at], (((1,), (1,)), ((), ())), preferred_element_type=F32
            )
            sums = term if sums is None else sums + term
        total[:, spot] = sums


def finish_kernel(flips, where, across, weight, total, *outs):
    row, column = where[2], where[3]
    width = across.shape[1]
    at = pl.ds(pl.multiple_of(jnp.bitwise_xor(column, 2) * width, width), width)
    for flip, out in zip(flips, outs):
        target = jnp.bitwise_xor(row, flip)
        spot = pl.ds(pl.multiple_of(target * width, width), width)
        term = lax.dot_general(
            across[...], weight[spot, at], (((1,), (1,)), ((), ())), preferred_element_type=F32
        )
        out[...] = (total[:, spot] + term).astype(out.dtype)


def earlier(value, steps):
    count = lax.axis_size("ctx")
    return lax.ppermute(value, "ctx", [(place, place - steps) for place in range(steps, count)])


def swapped(value, axis, flip):
    count = lax.axis_size(axis)
    return lax.ppermute(value, axis, [(place, place ^ flip) for place in range(count)])


def on_device(
    output_grad, conv_out, input_mix, output_mix, step_size, log_decay, skip_gain, conv_weight,
    later_grad, proj_weight,
):
    tokens, width = output_grad.shape
    heads = step_size.shape[0]
    states = input_mix.shape[2]
    part = HD // QUAD
    ctx, row, column = lax.axis_index("ctx"), lax.axis_index("row"), lax.axis_index("col")
    where = jnp.stack([ctx % QUAD, ctx // QUAD, row, column]).astype(jnp.int32)
    group = (row * lax.axis_size("col") + column) * heads // HPG
    reads = lax.dynamic_index_in_dim(output_mix, group, 1, keepdims=False)
    writes = lax.dynamic_index_in_dim(input_mix, group, 1, keepdims=False)
    later = later_grad.reshape(width, states)

    message = struct((heads * part + heads, states), BF16)
    piece = struct((heads, part, states), BF16)
    wide = struct((width, states), F32)
    plane = struct((tokens, width), F32)
    sums, cumulative, decays, *out = call(
        block_kernel,
        (wide, struct((heads, tokens), F32), struct((heads, states), F32)) + (message,) * 3,
        (where, output_grad, reads, log_decay),
        specs=(SMEM, HBM, VMEM, HBM),
        scratch=(
            pltpu.VMEM((tokens, width), BF16),
            pltpu.VMEM((heads, tokens), F32),
            pltpu.SemaphoreType.DMA((2,)),
        ),
    )
    near = [swapped(value, "ctx", flip) for flip, value in enumerate(out, 1)]
    quads = (
        pltpu.VMEM((QUAD, heads, part, states), F32),
        pltpu.VMEM((QUAD, heads, states), F32),
    )
    joined = call(
        quad_kernel, message, (where, sums, decays, *near, writes), specs=(SMEM,), scratch=quads,
    )
    far, middle, close = (earlier(joined, QUAD * ahead) for ahead in (3, 2, 1))
    fixed, slope, quarter = call(
        intra_kernel,
        (plane, plane, struct((heads, part, states), F32)),
        (where, skip_gain, output_grad, conv_out, step_size, later, writes, reads, cumulative)
        + (joined,),
        specs=(SMEM, SMEM, HBM, HBM, HBM, HBM),
        scratch=(
            pltpu.VMEM((tokens, tokens), F32),
            pltpu.VMEM((tokens, width), F32),
            pltpu.VMEM((tokens, width), BF16),
            pltpu.VMEM((tokens, width), BF16),
            pltpu.VMEM((heads, tokens), F32),
            pltpu.VMEM((width, states), F32),
            pltpu.SemaphoreType.DMA((4,)),
        ),
    )
    own, *out = call(
        carry_kernel,
        (piece,) * 4,
        (where, sums, decays, *near, middle, close, far, quarter),
        specs=(SMEM,),
        scratch=quads + (pltpu.VMEM((QUAD, heads, part, states), BF16),),
    )
    parts = [swapped(value, "ctx", flip) for flip, value in enumerate(out, 1)]
    blocks = [struct((count, width), BF16) for count in (FIRST, tokens - FIRST)]
    head, rim, rest, carried = call(
        join_kernel,
        (blocks[0], struct((8, width), BF16), blocks[1], struct((width, states), BF16)),
        (where, own, *parts, writes, fixed, slope, conv_weight),
        specs=(SMEM,),
        scratch=(pltpu.VMEM((FIRST + 16, width), F32),),
    )
    last = call(
        tail_kernel,
        blocks[1],
        (rest, earlier(rim, 1), conv_weight),
        scratch=(pltpu.VMEM((tokens - FIRST + 8, width), F32),),
    )
    sums_of, after = [], head
    for chunk in (head, last):
        near, far, across = (swapped(chunk, "col", flip) for flip in (1, 3, 2))
        block, held = struct(chunk.shape, BF16), struct(chunk.shape, F32)
        partial = call(
            product_kernel,
            struct((chunk.shape[0], proj_weight.shape[0]), F32),
            (where, chunk, far, near, proj_weight, after),
            specs=(SMEM,),
        )
        near, far = call(
            functools.partial(finish_kernel, (1, 3)),
            (block, block),
            (where, across, proj_weight, partial),
            specs=(SMEM,),
        )
        over, kept = call(
            functools.partial(finish_kernel, (2, 0)),
            (block, held),
            (where, across, proj_weight, partial),
            specs=(SMEM,),
        )
        came = [swapped(value, "row", flip) for value, flip in ((far, 3), (near, 1), (over, 2))]
        sums_of.append((kept, *came))
        after = kept
    state, x_grad = call(
        output_kernel,
        (wide, struct((tokens, width), BF16)),
        (sums, decays, carried, head, last, came[0]),
    )
    kept, *came = sums_of[-1]
    sums_of[-1] = lax.optimization_barrier((kept, *came, state))[:-1]
    sums_of = [kept + sum(value.astype(F32) for value in came) for kept, *came in sums_of]
    hidden_grad = jnp.concatenate(sums_of, axis=0).astype(BF16)
    return hidden_grad, x_grad, state.reshape(1, heads, HD, states)


def solution(mesh):
    return jax.shard_map(
        on_device,
        mesh=mesh,
        in_specs=(
            P("ctx", ("row", "col")),
            P("ctx", ("row", "col")),
            P("ctx", None, None),
            P("ctx", None, None),
            P(("row", "col"), "ctx"),
            P(("row", "col"), "ctx"),
            P(("row", "col")),
            P(None, ("row", "col")),
            P(("row", "col"), None, None),
            P("col", "row"),
        ),
        out_specs=(
            P("ctx", ("col", "row")),
            P("ctx", ("row", "col")),
            P("ctx", ("row", "col"), None, None),
        ),
        check_vma=False,
    )
```
